768 devices in a mesh: panel: 2 (over core), lat: 12 (over z), lon: 32 (over y, x).
Axes of the slice: x: 4, y: 8, z: 12, core: 2. Of those that a mesh axis runs over, the one named last changes fastest.
Arguments:
- tracers: float32 [2, 4, 8, 96, 4096], P('panel', None, None, 'lat', 'lon'), may hold values from 0.2 to 4
- courant_lon: float32 [2, 8, 96, 4096], P('panel', None, 'lat', 'lon'), may hold values from -0.45 to 0.45
- courant_lat: float32 [2, 8, 96, 4096], P('panel', None, 'lat', 'lon'), may hold values from -0.45 to 0.45
- cell_mass: float32 [2, 8, 96, 4096], P('panel', None, 'lat', 'lon'), as said below
- donor_cell: int32 [2, 12, 32, 12, 64], P('panel', 'lat', 'lon'), may hold values from 0 to 636, as said below
- donor_frac: float32 [2, 2, 12, 32, 12, 64], P(None, 'panel', 'lat', 'lon'), may hold values from 0 to 1
- target_cell: int32 [2, 12, 32, 12, 64], P('panel', 'lat', 'lon'), may hold values from 0 to 1023, as said below
- live_count: int32 [2, 12, 32, 12], P('panel', 'lat', 'lon'), may hold values from 0 to 64, as said below
Outputs:
- updated: float32 [2, 4, 8, 96, 4096], P('panel', None, None, 'lat', 'lon')
The draws below stay inside these ranges and needn't reach their ends.
Inputs may be any that keep to these rules, and one draw needn't show every extreme that they name: `donor_cell`: entry [p, a, b, d, k] is r * 128 + c with 0 <= r <= 4 and 0 <= c <= 124, so the whole stencil lies in the block of (p, a, b). `target_cell`: entry [p, d, b, s, k] is a flattened cell of the block of (p, d, b); the 768 entries of one device are all distinct. `live_count`: slots k >= the count carry nothing. `cell_mass`: the cell masses are positive.
All inputs are finite; a program needn't handle non-finite values.
Results may differ from the reference program's by a relative error of at most 0.0003.
Values sent between devices are 32-bit elements; how exact they have to be, the bound alone decides.
A program may use at most 32 MiB of HBM per device.

```python
import jax
import jax.numpy as jnp
from jax import lax

TRACERS = 4
LEVELS = 8
ROWS_DEV = 8
COLS_DEV = 128
SLOTS = 64
LAT_CELLS = 96
LON_CELLS = 4096
N_LAT = 12
N_LON = 32


def draw_tracers(key, part):
    shape = (2, TRACERS, LEVELS, N_LAT * ROWS_DEV, N_LON * COLS_DEV)
    first_key = jax.random.fold_in(jax.random.fold_in(key, 3), 0)
    panel_factor = 1.0 + lax.broadcasted_iota(jnp.float32, shape, 0)
    base = jax.random.uniform(first_key, shape, jnp.float32, 0.2, 2.0)
    return (base * panel_factor).astype(jnp.float32)


def draw_cell_mass(key, part):
    shape = (2, LEVELS, N_LAT * ROWS_DEV, N_LON * COLS_DEV)
    first_key = jax.random.fold_in(jax.random.fold_in(key, 5), 0)
    row_share = lax.broadcasted_iota(jnp.float32, shape, 2) / (N_LAT * ROWS_DEV - 1)
    panel_factor = 2.0 - lax.broadcasted_iota(jnp.float32, shape, 0)
    ramp = (1.0 + 2.0 * row_share) * panel_factor
    factor = jnp.exp(jax.random.uniform(first_key, shape, jnp.float32, jnp.log(0.5), jnp.log(2.0)))
    return (factor * ramp).astype(jnp.float32)


def draw_donor_cell(key, part):
    row_key, column_key = jax.random.split(jax.random.fold_in(key, 11))
    shape = (2, N_LAT, N_LON, N_LAT, SLOTS)
    row_start = jax.random.randint(row_key, shape, 0, ROWS_DEV - 3)
    column_start = jax.random.randint(column_key, shape, 0, COLS_DEV - 3)
    return (row_start * COLS_DEV + column_start).astype(jnp.int32)


def draw_target_cell(key, part):
    device_keys = jax.random.split(jax.random.fold_in(key, 23), 2 * N_LAT * N_LON)
    orders = jax.vmap(lambda single: jax.random.permutation(single, ROWS_DEV * COLS_DEV)[:N_LAT * SLOTS])(device_keys)
    return orders.reshape(2, N_LAT, N_LON, N_LAT, SLOTS).astype(jnp.int32)


def draw_live_count(key, part):
    high_key, low_key = jax.random.split(jax.random.fold_in(key, 37))
    shape = (2, N_LAT, N_LON, N_LAT)
    row_place = lax.broadcasted_iota(jnp.int32, shape, 1)
    column_place = lax.broadcasted_iota(jnp.int32, shape, 2)
    edge_row = (row_place == 0) | (row_place == N_LAT - 1)
    edge_column = (column_place == 0) | (column_place == N_LON - 1)
    high_count = jax.random.randint(high_key, shape, SLOTS // 4, SLOTS + 1)
    low_count = jax.random.randint(low_key, shape, 0, SLOTS // 4 + 1)
    return jnp.where(edge_row, SLOTS, jnp.where(edge_column, high_count, low_count)).astype(jnp.int32)


def shard_levels(own_key, dims, pieces, low, high):
    gain, own = 1.0, jax.random.fold_in(own_key, 6)
    for axis_at, parts in pieces:
        heights = jnp.exp(jax.random.uniform(jax.random.fold_in(own, axis_at), (parts,), jnp.float32, low / len(pieces), high / len(pieces)))
        gain = gain * jnp.repeat(heights, dims[axis_at] // parts).reshape([-1 if axis == axis_at else 1 for axis in range(len(dims))])
    return gain


def setup_inputs(seed: int = 0) -> dict:
    streams_of = jax.random.split(jax.random.key(seed), 9)
    tracers = draw_tracers(jax.random.fold_in(streams_of[8], 71), 0)
    courant_lon = jnp.clip(jax.random.uniform(streams_of[1], (2, LEVELS, LAT_CELLS, LON_CELLS), jnp.float32, -0.45, 0.45) * shard_levels(streams_of[1], (2, LEVELS, LAT_CELLS, LON_CELLS), ((0, 2), (2, 12), (3, 32)), -0.4, 0.0), -0.45, 0.45)
    courant_lat = jnp.clip(jax.random.uniform(streams_of[2], (2, LEVELS, LAT_CELLS, LON_CELLS), jnp.float32, -0.45, 0.45) * shard_levels(streams_of[2], (2, LEVELS, LAT_CELLS, LON_CELLS), ((0, 2), (2, 12), (3, 32)), -0.4, 0.0), -0.45, 0.45)
    cell_mass = draw_cell_mass(jax.random.fold_in(streams_of[8], 71), 0)
    donor_cell = draw_donor_cell(jax.random.fold_in(streams_of[8], 71), 0)
    donor_frac = jnp.clip(1.0 * jax.random.uniform(streams_of[5], (2, 2, N_LAT, N_LON, N_LAT, SLOTS), jnp.float32) ** shard_levels(streams_of[5], (2, 2, N_LAT, N_LON, N_LAT, SLOTS), ((1, 2), (2, 12), (3, 32)), -0.2, 0.2), 0.0, 1.0)
    target_cell = draw_target_cell(jax.random.fold_in(streams_of[8], 71), 0)
    live_count = draw_live_count(jax.random.fold_in(streams_of[8], 71), 0)
    return {"tracers": tracers, "courant_lon": courant_lon, "courant_lat": courant_lat, "cell_mass": cell_mass, "donor_cell": donor_cell, "donor_frac": donor_frac, "target_cell": target_cell, "live_count": live_count}


def cut(source, begin_at, end_at, dim_index):
    return lax.slice_in_dim(source, begin_at, end_at, axis=dim_index)


def face_flux(padded_field, courant, length, from_end):
    dim_index = padded_field.ndim - from_end
    edge_values = (7.0 / 12.0) * (cut(padded_field, 1, length + 4, dim_index) + cut(padded_field, 2, length + 5, dim_index)) - (1.0 / 12.0) * (cut(padded_field, 0, length + 3, dim_index) + cut(padded_field, 3, length + 6, dim_index))
    edge_left = cut(edge_values, 0, length + 1, dim_index)
    edge_middle = cut(edge_values, 1, length + 2, dim_index)
    edge_right = cut(edge_values, 2, length + 3, dim_index)
    cell_left = cut(padded_field, 2, length + 3, dim_index)
    cell_right = cut(padded_field, 3, length + 4, dim_index)
    number = cut(courant, 3, length + 4, dim_index)
    slope_left = edge_middle - edge_left
    curve_left = 6.0 * (cell_left - 0.5 * (edge_left + edge_middle))
    flux_positive = number * (edge_middle - 0.5 * number * (slope_left - (1.0 - (2.0 / 3.0) * number) * curve_left))
    reverse_speed = -number
    slope_right = edge_right - edge_middle
    curve_right = 6.0 * (cell_right - 0.5 * (edge_middle + edge_right))
    flux_negative = number * (edge_middle + 0.5 * reverse_speed * (slope_right + (1.0 - (2.0 / 3.0) * reverse_speed) * curve_right))
    return jnp.where(number > 0.0, flux_positive, flux_negative)


def advect(padded_field, zonal_padded, meridional_padded):
    row_total = padded_field.shape[-2] - 6
    column_total = padded_field.shape[-1] - 6
    zonal_flux = face_flux(padded_field[..., 3:3 + row_total, :], zonal_padded[..., 3:3 + row_total, :], column_total, 1)
    meridional_flux = face_flux(padded_field[..., 3:3 + column_total], meridional_padded[..., 3:3 + column_total], row_total, 2)
    center = padded_field[..., 3:3 + row_total, 3:3 + column_total]
    return center - (zonal_flux[..., 1:] - zonal_flux[..., :-1]) - (meridional_flux[..., 1:, :] - meridional_flux[..., :-1, :])


def cubic_weights(fraction):
    return jnp.stack([-fraction * (fraction - 1.0) * (fraction - 2.0) / 6.0, (fraction + 1.0) * (fraction - 1.0) * (fraction - 2.0) / 2.0, -(fraction + 1.0) * fraction * (fraction - 2.0) / 2.0, (fraction + 1.0) * fraction * (fraction - 1.0) / 6.0], axis=-1)


def interpolate(flat_field, base_cell, fraction_row, fraction_column, column_total):
    row_weights = cubic_weights(fraction_row)
    column_weights = cubic_weights(fraction_column)
    total = jnp.zeros((flat_field.shape[0], base_cell.shape[0]), jnp.float32)
    for step_row in range(4):
        for step_column in range(4):
            spots = (base_cell + step_row * column_total + step_column).astype(jnp.int32)
            factor = row_weights[:, step_row] * column_weights[:, step_column]
            total = total + factor[None, :] * jnp.take(flat_field, spots, axis=1)
    return total


def reference(tracers, courant_lon, courant_lat, cell_mass, donor_cell, donor_frac, target_cell, live_count):
    pad_widths = ((0, 0), (0, 0), (3, 3), (3, 3))
    zonal_padded = jnp.pad(courant_lon, pad_widths)
    meridional_padded = jnp.pad(courant_lat, pad_widths)

    def one_tracer(tracer_field):
        return advect(jnp.pad(tracer_field, pad_widths), zonal_padded, meridional_padded)

    advected = jnp.moveaxis(lax.map(one_tracer, jnp.moveaxis(tracers, 1, 0)), 0, 1)
    stack_rows = TRACERS * LEVELS
    cell_total = ROWS_DEV * COLS_DEV
    device_total = 2 * N_LAT * N_LON
    slot_total = N_LAT * SLOTS
    blocks = advected.reshape(2, stack_rows, N_LAT, ROWS_DEV, N_LON, COLS_DEV).transpose(0, 2, 4, 1, 3, 5).reshape(device_total, stack_rows, cell_total)

    def donate(member):
        flat_field, base_cell, fraction_row, fraction_column = member
        return interpolate(flat_field, base_cell, fraction_row, fraction_column, COLS_DEV)

    interpolated = lax.map(donate, (blocks, donor_cell.reshape(device_total, slot_total), donor_frac[0].reshape(device_total, slot_total), donor_frac[1].reshape(device_total, slot_total))).transpose(0, 2, 1)
    arrived = interpolated.reshape(2, N_LAT, N_LON, N_LAT, SLOTS, stack_rows)[::-1].transpose(0, 3, 2, 1, 4, 5).reshape(device_total, slot_total, stack_rows)
    slot_index = jnp.arange(SLOTS, dtype=jnp.int32)
    live_slots = slot_index[None, None, None, None, :] < live_count[..., None]
    targets = jnp.where(live_slots, target_cell, cell_total).reshape(device_total, slot_total).astype(jnp.int32)

    def receive(member):
        flat_field, values_in, target_spots = member
        return flat_field.at[:, target_spots].set(values_in.T, mode="drop")

    merged = lax.map(receive, (blocks, arrived, targets))
    intersected = merged.reshape(2, N_LAT, N_LON, TRACERS, LEVELS, ROWS_DEV, COLS_DEV).transpose(0, 3, 4, 1, 5, 2, 6).reshape(2, TRACERS, LEVELS, N_LAT * ROWS_DEV, N_LON * COLS_DEV)
    mass_old = jnp.sum(cell_mass[:, None] * tracers, axis=(0, 2, 3, 4))
    mass_new = jnp.sum(cell_mass[:, None] * intersected, axis=(0, 2, 3, 4))
    return intersected * (mass_old / mass_new)[None, :, None, None, None]
```

```python
import jax
import jax.numpy as jnp
from jax import lax
from jax.experimental import pallas as pl
from jax.experimental.pallas import tpu as pltpu
from jax.sharding import PartitionSpec as P

F32 = jnp.float32
BF16 = jnp.bfloat16
MESH = pl.DeviceIdType.MESH

T = 4
L = 8
F = T * L
R = 8
C = 128
K = 64
NX = 4
WEST, EAST, SOUTH, NORTH, NORTH_C, MASSES, MARGIN, SUM_X, SUM_Y, SUM_Z = range(10)


def left(x, by):
    by = by % C
    return x if by == 0 else pltpu.roll(x, (C - by) % C, x.ndim - 1)


def alphas(c):
    s = jnp.abs(c)
    m = 0.5 * s
    n = m - m * s * (2.0 / 3.0)
    n3 = 3.0 * n
    k1 = c * (1.0 - m - n3)
    k0 = c * (m - n3)
    ka = 2.0 * n3 * c
    u = k0 * (1.0 / 12.0)
    w = k1 * (1.0 / 12.0)
    pos = c > 0.0
    zero = jnp.zeros_like(c)
    near = 7.0 * (u + w) + ka
    far = 7.0 * u - w
    mid = 7.0 * w - u
    return (
        jnp.where(pos, -u, zero),
        jnp.where(pos, far, -w),
        jnp.where(pos, near, mid),
        jnp.where(pos, mid, near),
        jnp.where(pos, -w, far),
        jnp.where(pos, zero, -u),
    )


def betas(c, c_next):
    here, after = alphas(c), alphas(c_next)
    return [-here[0]] + [after[k - 1] - here[k] for k in range(1, 6)] + [after[5]]


def cubic(t):
    a, b, d = t + 1.0, t - 1.0, t - 2.0
    return (
        -t * b * d * (1.0 / 6.0),
        a * b * d * 0.5,
        -a * t * d * 0.5,
        a * t * b * (1.0 / 6.0),
    )


def pick(delta, weights):
    value = jnp.where(delta == 0, weights[0], 0.0)
    for i in range(1, 4):
        value = jnp.where(delta == i, weights[i], value)
    return value


def halves(x):
    high = x.astype(BF16)
    return high, (x - high.astype(F32)).astype(BF16)


def wait_all(ref, sem):
    pltpu.make_async_copy(ref, ref, sem).wait()


def kernel(nz, nlon, q_hbm, clon_hbm, clat_hbm, mass_hbm, donor_hbm, frac_hbm, target_hbm, live,
           out, field, clon, clat, mass, donor, frac, target, send_w, send_e, recv_w, recv_e,
           cm_send, cm_recv, packet, arrived, rows, sum_x, sum_y, sum_z, base, adv, onehot, colw,
           roww, lhs, mixed, scat_hi, scat_lo, rowmask, scattered, local_sem, send_sem, recv_sem):
    p = lax.axis_index("panel")
    z = lax.axis_index("lat")
    b = lax.axis_index("lon")
    x, y = lax.rem(b, NX), lax.div(b, NX)
    ny = nlon // NX
    other = 1 - p

    def at_z(step):
        return lax.rem(z + step, nz)

    def at_x(step):
        return y * NX + lax.rem(x + step, NX)

    def at_y(step):
        return lax.rem(y + step, ny) * NX + x

    west, east = lax.rem(b + nlon - 1, nlon), lax.rem(b + 1, nlon)
    south, north = at_z(nz - 1), at_z(1)

    loads = [
        pltpu.make_async_copy(q_hbm, field.at[:, pl.ds(R, R), :], local_sem.at[0]),
        pltpu.make_async_copy(clon_hbm, clon, local_sem.at[1]),
        pltpu.make_async_copy(clat_hbm, clat.at[:, pl.ds(0, R), :], local_sem.at[2]),
        pltpu.make_async_copy(mass_hbm, mass, local_sem.at[3]),
        pltpu.make_async_copy(donor_hbm, donor, local_sem.at[4]),
        pltpu.make_async_copy(frac_hbm, frac, local_sem.at[5]),
        pltpu.make_async_copy(target_hbm, target, local_sem.at[6]),
    ]
    barrier = pltpu.get_barrier_semaphore()
    partners = [(other, at_z(i), b) for i in range(nz)] + [(p, at_z(i), b) for i in range(1, nz)]
    partners += [(p, z, west), (p, z, east)]
    partners += [(core, z, at_x(i)) for i in range(1, NX) for core in (p, other)]
    partners += [(p, z, at_y(i)) for i in range(1, ny)]
    for partner in partners:
        pl.semaphore_signal(barrier, inc=1, device_id=partner, device_id_type=MESH)
    for load in loads:
        load.start()

    lane = lax.broadcasted_iota(jnp.int32, (R, C), 1)
    lane16 = lax.broadcasted_iota(jnp.int32, (2 * R, C), 1)
    lane_row = lax.broadcasted_iota(jnp.int32, (1, C), 1)
    sub = lax.broadcasted_iota(jnp.int32, (2 * R, C), 0)
    column = lax.broadcasted_iota(jnp.int32, (C, C), 0)
    low, low16 = lane < K, lane16 < K

    loads[6].wait()
    spots = jnp.concatenate([target[0:6, :], target[6:12, :]], axis=1)
    spot_col = spots & (C - 1)
    spot_row = spots >> 7
    live_rows = []
    for v in range(6):
        count = jnp.where(lane_row < K, live[v], live[v + 6])
        live_rows.append(jnp.where((lane_row & (K - 1)) < count, spot_row[v : v + 1, :], R))
    for v in range(6):
        cols = pl.ds(v * C, C)
        onehot[:, cols] = jnp.where(column == spot_col[v : v + 1, :], 1.0, 0.0).astype(BF16)
        rowmask[:, cols] = jnp.where(sub == live_rows[v], 1.0, 0.0).astype(BF16)
    filled = lax.dot_general(
        rowmask[...], onehot[...], (((1,), (1,)), ((), ())), preferred_element_type=F32
    )[0:R, :]

    loads[3].wait()
    by_row = jnp.concatenate([mass[pl.ds(r, L, stride=R), :] for r in range(R)], axis=0)
    mass_hi, mass_lo = halves(by_row)
    mass_at = jnp.dot(mass_hi, onehot[...], preferred_element_type=F32) + jnp.dot(
        mass_lo, onehot[...], preferred_element_type=F32
    )
    for v in range(6):
        total = jnp.zeros((L, C), F32)
        for r in range(R):
            total += jnp.where(
                live_rows[v] == r, mass_at[r * L : (r + 1) * L, v * C : (v + 1) * C], 0.0
            )
        turned = left(total, K)
        cm_send[v] = jnp.where(low, total, pltpu.roll(turned, 4, 0))[0:4, :]
        cm_send[v + 6] = jnp.where(low, turned, pltpu.roll(total, 4, 0))[0:4, :]

    loads[0].wait()
    loads[1].wait()
    own = [jnp.zeros((R, C), F32) for _ in range(4)]
    firsts = (0, 4, 124, 120)
    for f in range(F):
        tile = field[f, R : 2 * R, :]
        band = (lane >= 4 * f) & (lane < 4 * f + 4)
        own = [jnp.where(band, left(tile, first - 4 * f), o) for first, o in zip(firsts, own)]
    own_w, own_w2, own_e, own_e2 = own
    edge = [jnp.zeros((R, C), F32) for _ in range(4)]
    firsts = (0, 1, 124, 125)
    for l in range(L):
        tile = clon[l]
        band = (lane >= 4 * l) & (lane < 4 * l + 4)
        edge = [jnp.where(band, left(tile, first - 4 * l), o) for first, o in zip(firsts, edge)]
    edge = [o + pltpu.roll(o, 32, 1) for o in edge]
    c_w, c_w_next, c_e, c_e_next = [o + pltpu.roll(o, 64, 1) for o in edge]
    send_w[0] = own_w
    send_w[1] = c_w
    send_e[0] = own_e

    loads[4].wait()
    loads[5].wait()
    cells = jnp.concatenate([donor[0:6, :], donor[6:12, :]], axis=1)
    start_col = cells & (C - 1)
    start_row = cells >> 7
    row_weights = cubic(jnp.concatenate([frac[0, 0:6, :], frac[0, 6:12, :]], axis=1))
    col_weights = cubic(jnp.concatenate([frac[1, 0:6, :], frac[1, 6:12, :]], axis=1))
    for r in range(R):
        roww[r, 0:6, :] = pick(r - start_row, row_weights)
    for v in range(6):
        cols = pl.ds(v * C, C)
        weights = pick(
            column - start_col[v : v + 1, :], [w[v : v + 1, :] for w in col_weights]
        )
        high, low_part = halves(weights)
        colw[0:C, cols] = high
        colw[C : 2 * C, cols] = high
        colw[2 * C : 3 * C, cols] = low_part

    pl.semaphore_wait(barrier, len(partners))

    def remote(src, dst, which, device):
        return pltpu.make_async_remote_copy(
            src_ref=src,
            dst_ref=dst,
            send_sem=send_sem.at[which],
            recv_sem=recv_sem.at[which],
            device_id=device,
            device_id_type=MESH,
        )

    halo = [
        remote(send_w, recv_e, EAST, (p, z, west)),
        remote(send_e, recv_w, WEST, (p, z, east)),
        remote(q_hbm.at[:, pl.ds(5, 3), :], field.at[:, pl.ds(5, 3), :], SOUTH, (p, north, b)),
        remote(q_hbm.at[:, pl.ds(0, 3), :], field.at[:, pl.ds(16, 3), :], NORTH, (p, south, b)),
        remote(clat_hbm.at[:, pl.ds(0, 1), :], clat.at[:, pl.ds(R, 1), :], NORTH_C, (p, south, b)),
    ]
    for copy in halo:
        copy.start()
    far_first = sorted(range(nz), key=lambda i: -min(i, nz - i))
    for i in far_first:
        peer = at_z(i)
        remote(cm_send.at[peer], cm_recv.at[z], MASSES, (other, peer, b)).start()

    loads[2].wait()
    inside = (lane >= 4) & (lane < 124)
    mass_old = [jnp.zeros((R, C), F32) for _ in range(T)]
    for l in range(L):
        coef = [
            jnp.where(inside, o, 0.0) for o in betas(clon[l], left(clon[l], 1))
        ]
        for t in range(T):
            tile = field[t * L + l, R : 2 * R, :]
            mass_old[t] += mass[l * R : (l + 1) * R, :] * tile
            value = tile
            for k in range(7):
                value -= coef[k] * left(tile, k - 3)
            base[t * L + l] = value

    for copy in halo[:2]:
        copy.wait()
    quarter = lane & 3
    halo_w = jnp.where(b == 0, 0.0, recv_w[0])
    halo_e = jnp.where(b == nlon - 1, 0.0, recv_e[0])
    halo_c = jnp.where(b == nlon - 1, 0.0, recv_e[1])
    c_e_next = jnp.where(quarter == 3, left(halo_c, -3), c_e_next)

    def packed(before, middle, after, coef):
        value = coef[3] * middle
        for k in range(7):
            s = k - 3
            if s < 0:
                cell = jnp.where(quarter < -s, left(before, 4 + s), left(middle, s))
            elif s > 0:
                cell = jnp.where(quarter >= 4 - s, left(after, s - 4), left(middle, s))
            else:
                continue
            value += coef[k] * cell
        return value

    change_w = packed(halo_w, own_w, own_w2, betas(c_w, c_w_next))
    change_e = packed(own_e2, own_e, halo_e, betas(c_e, c_e_next))

    for copy in halo[2:]:
        copy.wait()

    @pl.when(z == 0)
    def _():
        field[:, 5:8, :] = jnp.zeros((F, 3, C), F32)

    @pl.when(z == nz - 1)
    def _():
        field[:, 16:19, :] = jnp.zeros((F, 3, C), F32)
        clat[:, 8:9, :] = jnp.zeros((L, 1, C), F32)

    keep = filled < 0.5
    mass_new = [jnp.zeros((R, C), F32) for _ in range(T)]
    for l in range(L):
        coef = betas(clat[l, 0:8, :], clat[l, 1:9, :])
        kept = jnp.where(keep, mass[l * R : (l + 1) * R, :], 0.0)
        for t in range(T):
            f = t * L + l
            value = base[f]
            value -= jnp.where(lane < 4, left(change_w, 4 * f), 0.0)
            value -= jnp.where(lane >= 124, left(change_e, 4 * f + 4), 0.0)
            for k in range(7):
                value -= coef[k] * field[f, 5 + k : 13 + k, :]
            adv[f * R : (f + 1) * R, :] = value
            mass_new[t] += kept * value

    for r in range(R):
        high, low_part = halves(adv[pl.ds(r, F, stride=R), :])
        at = pl.ds(r * F, F)
        lhs[at, 0:C] = high
        lhs[at, C : 2 * C] = low_part
        lhs[at, 2 * C : 3 * C] = high
    mixed[...] = jnp.dot(lhs[...], colw[...], preferred_element_type=F32)
    for v in range(6):
        total = jnp.zeros((F, C), F32)
        for r in range(R):
            total += roww[r, v : v + 1, :] * mixed[r * F : (r + 1) * F, v * C : (v + 1) * C]
        first, second = total[0 : F // 2, :], total[F // 2 : F, :]
        packet[v] = jnp.where(low16, first, left(second, K))
        packet[v + 6] = jnp.where(low16, left(first, K), second)
    for i in far_first:
        peer = at_z(i)
        remote(packet.at[peer], arrived.at[z], MARGIN, (other, peer, b)).start()

    wait_all(cm_recv, recv_sem.at[MASSES])
    parts = [jnp.zeros((R, C), F32) for _ in range(2)]
    for d in range(12):
        four = cm_recv[d]
        eight = jnp.concatenate([four, left(four, K)], axis=0)
        eight = jnp.where(low, eight, left(eight, K))
        for half in range(2):
            parts[half] += eight * packet[d, half * R : (half + 1) * R, :]
    for half in range(2):
        mass_new[half] += jnp.where(low, parts[half], 0.0)
        mass_new[half + 2] += jnp.where(low, 0.0, parts[half])
    stacked = jnp.concatenate(
        [jnp.sum(m, axis=0, keepdims=True) for m in mass_old + mass_new], axis=0
    )
    sums = jnp.sum(stacked, axis=1, keepdims=True)
    row = jnp.sum(jnp.where(lane == sub[0:R, :], sums, 0.0), axis=0, keepdims=True)

    rows[0] = row
    group = [(other, z, b)]
    group += [(core, z, at_x(i)) for i in range(1, NX) for core in (p, other)]
    for i, device in enumerate(group):
        remote(rows.at[0], sum_x.at[i], SUM_X, device).start()
    wait_all(sum_x, recv_sem.at[SUM_X])
    row = row + jnp.sum(sum_x[...], axis=0)
    rows[1] = row
    for i in range(1, ny):
        remote(rows.at[1], sum_y.at[i - 1], SUM_Y, (p, z, at_y(i))).start()
    wait_all(sum_y, recv_sem.at[SUM_Y])
    row = row + jnp.sum(sum_y[...], axis=0)
    rows[2] = row
    for i in range(1, nz):
        remote(rows.at[2], sum_z.at[i - 1], SUM_Z, (p, at_z(i), b)).start()

    wait_all(arrived, recv_sem.at[MARGIN])
    for v in range(6):
        cols = pl.ds(v * C, C)
        one, two = arrived[v], arrived[v + 6]
        first = jnp.where(low16, one, left(two, K))
        second = jnp.where(low16, left(one, K), two)
        values = jnp.concatenate([first, second], axis=0)
        high = values.astype(BF16).astype(F32)
        low_part = values - high
        for r in range(R):
            at = pl.ds(r * F, F)
            here = live_rows[v] == r
            scat_hi[at, cols] = jnp.where(here, high, 0.0).astype(BF16)
            scat_lo[at, cols] = jnp.where(here, low_part, 0.0).astype(BF16)
    nt = (((1,), (1,)), ((), ()))
    scattered[...] = lax.dot_general(
        scat_hi[...], onehot[...], nt, preferred_element_type=F32
    ) + lax.dot_general(scat_lo[...], onehot[...], nt, preferred_element_type=F32)
    for f in range(F):
        at = pl.ds(f * R, R)
        adv[at, :] = jnp.where(keep, adv[at, :], scattered[pl.ds(f, R, stride=F), :])

    wait_all(sum_z, recv_sem.at[SUM_Z])
    row = row + jnp.sum(sum_z[...], axis=0)
    ratio = row / left(row, 4)
    for t in range(T):
        scale = jnp.broadcast_to(ratio[:, t : t + 1], (R, C))
        for l in range(L):
            f = t * L + l
            out[f] = adv[f * R : (f + 1) * R, :] * scale

    wait_all(cm_send, send_sem.at[MASSES])
    wait_all(packet, send_sem.at[MARGIN])
    wait_all(sum_x, send_sem.at[SUM_X])
    wait_all(sum_y, send_sem.at[SUM_Y])
    wait_all(sum_z, send_sem.at[SUM_Z])


def solution(mesh):
    nz, nlon = mesh.shape["lat"], mesh.shape["lon"]
    ny = nlon // NX

    def body(tracers, courant_lon, courant_lat, cell_mass, donor_cell, donor_frac, target_cell, live_count):
        slots = nz * K
        any_spec = pl.BlockSpec(memory_space=pl.ANY)

        def run(*refs):
            kernel(nz, nlon, *refs)

        result = pl.pallas_call(
            run,
            out_shape=jax.ShapeDtypeStruct((F, R, C), F32),
            in_specs=[any_spec] * 7 + [pl.BlockSpec(memory_space=pltpu.SMEM)],
            out_specs=pl.BlockSpec(memory_space=pltpu.VMEM),
            scratch_shapes=[
                pltpu.VMEM((F, 3 * R, C), F32),
                pltpu.VMEM((L, R, C), F32),
                pltpu.VMEM((L, 2 * R, C), F32),
                pltpu.VMEM((L * R, C), F32),
                pltpu.VMEM((nz, K), jnp.int32),
                pltpu.VMEM((2, nz, K), F32),
                pltpu.VMEM((nz, K), jnp.int32),
                pltpu.VMEM((2, R, C), F32),
                pltpu.VMEM((1, R, C), F32),
                pltpu.VMEM((1, R, C), F32),
                pltpu.VMEM((2, R, C), F32),
                pltpu.VMEM((nz, 4, C), F32),
                pltpu.VMEM((nz, 4, C), F32),
                pltpu.VMEM((nz, 2 * R, C), F32),
                pltpu.VMEM((nz, 2 * R, C), F32),
                pltpu.VMEM((3, 1, C), F32),
                pltpu.VMEM((2 * NX - 1, 1, C), F32),
                pltpu.VMEM((ny - 1, 1, C), F32),
                pltpu.VMEM((nz - 1, 1, C), F32),
                pltpu.VMEM((F, R, C), F32),
                pltpu.VMEM((F * R, C), F32),
                pltpu.VMEM((C, slots), BF16),
                pltpu.VMEM((3 * C, slots), BF16),
                pltpu.VMEM((R, R, C), F32),
                pltpu.VMEM((F * R, 3 * C), BF16),
                pltpu.VMEM((F * R, slots), F32),
                pltpu.VMEM((F * R, slots), BF16),
                pltpu.VMEM((F * R, slots), BF16),
                pltpu.VMEM((2 * R, slots), BF16),
                pltpu.VMEM((F * R, C), F32),
                pltpu.SemaphoreType.DMA((7,)),
                pltpu.SemaphoreType.DMA((10,)),
                pltpu.SemaphoreType.DMA((10,)),
            ],
            compiler_params=pltpu.CompilerParams(collective_id=0, has_side_effects=True),
        )(
            tracers.reshape(F, R, C),
            courant_lon.reshape(L, R, C),
            courant_lat.reshape(L, R, C),
            cell_mass.reshape(L * R, C),
            donor_cell.reshape(nz, K),
            donor_frac.reshape(2, nz, K),
            target_cell.reshape(nz, K),
            live_count.reshape(nz),
        )
        return result.reshape(1, T, L, R, C)

    lon = "lon"
    placed = (
        P("panel", None, None, "lat", lon),
        P("panel", None, "lat", lon),
        P("panel", None, "lat", lon),
        P("panel", None, "lat", lon),
        P("panel", "lat", lon, None, None),
        P(None, "panel", "lat", lon, None, None),
        P("panel", "lat", lon, None, None),
        P("panel", "lat", lon, None),
    )
    return jax.shard_map(
        body,
        mesh=mesh,
        in_specs=placed,
        out_specs=P("panel", None, None, "lat", lon),
        check_vma=False,
    )
```

```python
import jax
import jax.numpy as jnp
from jax import lax
from jax.experimental import pallas as pl
from jax.experimental.pallas import tpu as pltpu
from jax.sharding import PartitionSpec as P

F32 = jnp.float32
BF16 = jnp.bfloat16
MESH = pl.DeviceIdType.MESH

T = 4
L = 8
F = T * L
R = 8
C = 128
K = 64
NX = 4
WEST, EAST, SOUTH, NORTH, NORTH_C, MASSES, MARGIN, SUM_X, SUM_Y, SUM_Z = range(10)


def left(x, by):
    by = by % C
    return x if by == 0 else pltpu.roll(x, (C - by) % C, x.ndim - 1)


def alphas(c):
    s = jnp.abs(c)
    m = 0.5 * s
    n = m - m * s * (2.0 / 3.0)
    n3 = 3.0 * n
    k1 = c * (1.0 - m - n3)
    k0 = c * (m - n3)
    ka = 2.0 * n3 * c
    u = k0 * (1.0 / 12.0)
    w = k1 * (1.0 / 12.0)
    pos = c > 0.0
    zero = jnp.zeros_like(c)
    near = 7.0 * (u + w) + ka
    far = 7.0 * u - w
    mid = 7.0 * w - u
    return (
        jnp.where(pos, -u, zero),
        jnp.where(pos, far, -w),
        jnp.where(pos, near, mid),
        jnp.where(pos, mid, near),
        jnp.where(pos, -w, far),
        jnp.where(pos, zero, -u),
    )


def betas(c, c_next):
    here, after = alphas(c), alphas(c_next)
    return [-here[0]] + [after[k - 1] - here[k] for k in range(1, 6)] + [after[5]]


def cubic(t):
    a, b, d = t + 1.0, t - 1.0, t - 2.0
    return (
        -t * b * d * (1.0 / 6.0),
        a * b * d * 0.5,
        -a * t * d * 0.5,
        a * t * b * (1.0 / 6.0),
    )


def pick(delta, weights):
    value = jnp.where(delta == 0, weights[0], 0.0)
    for i in range(1, 4):
        value = jnp.where(delta == i, weights[i], value)
    return value


def halves(x):
    high = x.astype(BF16)
    return high, (x - high.astype(F32)).astype(BF16)


def wait_all(ref, sem):
    pltpu.make_async_copy(ref, ref, sem).wait()


def kernel(nz, nlon, q_hbm, clon_hbm, clat_hbm, mass_hbm, donor_hbm, frac_hbm, target_hbm, live_hbm,
           out, scale_out, field, clon, clat, mass, donor, frac, target, live, send_w, send_e, recv_w, recv_e,
           cm_send, cm_recv, packet, arrived, rows, sum_x, sum_y, sum_z, base, adv, onehot, colw,
           roww, lhs, mixed, scat_hi, scat_lo, rowmask, scattered, local_sem, send_sem, recv_sem):
    p = lax.axis_index("panel")
    z = lax.axis_index("lat")
    b = lax.axis_index("lon")
    x, y = lax.rem(b, NX), lax.div(b, NX)
    ny = nlon // NX
    other = 1 - p

    def at_z(step):
        return lax.rem(z + step, nz)

    def at_x(step):
        return y * NX + lax.rem(x + step, NX)

    def at_y(step):
        return lax.rem(y + step, ny) * NX + x

    west, east = lax.rem(b + nlon - 1, nlon), lax.rem(b + 1, nlon)
    south, north = at_z(nz - 1), at_z(1)

    loads = [
        pltpu.make_async_copy(q_hbm, field.at[:, pl.ds(R, R), :], local_sem.at[0]),
        pltpu.make_async_copy(clon_hbm, clon, local_sem.at[1]),
        pltpu.make_async_copy(clat_hbm, clat.at[:, pl.ds(0, R), :], local_sem.at[2]),
        pltpu.make_async_copy(mass_hbm, mass, local_sem.at[3]),
        pltpu.make_async_copy(donor_hbm, donor, local_sem.at[4]),
        pltpu.make_async_copy(frac_hbm, frac, local_sem.at[5]),
        pltpu.make_async_copy(target_hbm, target, local_sem.at[6]),
        pltpu.make_async_copy(live_hbm, live, local_sem.at[7]),
    ]
    barrier = pltpu.get_barrier_semaphore()
    partners = [(other, at_z(i), b) for i in range(nz)] + [(p, at_z(i), b) for i in range(1, nz)]
    partners += [(p, z, west), (p, z, east)]
    partners += [(core, z, at_x(i)) for i in range(1, NX) for core in (p, other)]
    partners += [(p, z, at_y(i)) for i in range(1, ny)]
    for partner in partners:
        pl.semaphore_signal(barrier, inc=1, device_id=partner, device_id_type=MESH)
    for load in loads:
        load.start()

    lane = lax.broadcasted_iota(jnp.int32, (R, C), 1)
    lane16 = lax.broadcasted_iota(jnp.int32, (2 * R, C), 1)
    lane_row = lax.broadcasted_iota(jnp.int32, (1, C), 1)
    sub = lax.broadcasted_iota(jnp.int32, (2 * R, C), 0)
    column = lax.broadcasted_iota(jnp.int32, (C, C), 0)
    low, low16 = lane < K, lane16 < K

    loads[6].wait()
    loads[7].wait()

    def slots(read):
        return jnp.concatenate(
            [jnp.concatenate([read(v), read(v + 6)], axis=1) for v in range(6)], axis=0
        )

    spots = slots(lambda d: target[d])
    spot_col = spots & (C - 1)
    spot_row = spots >> 7
    live_rows = []
    for v in range(6):
        count = jnp.where(lane_row < K, live[v], live[v + 6])
        live_rows.append(jnp.where((lane_row & (K - 1)) < count, spot_row[v : v + 1, :], R))
    for v in range(6):
        cols = pl.ds(v * C, C)
        onehot[:, cols] = jnp.where(column == spot_col[v : v + 1, :], 1.0, 0.0).astype(BF16)
        rowmask[:, cols] = jnp.where(sub == live_rows[v], 1.0, 0.0).astype(BF16)
    filled = lax.dot_general(
        rowmask[...], onehot[...], (((1,), (1,)), ((), ())), preferred_element_type=F32
    )[0:R, :]

    loads[3].wait()
    by_row = jnp.concatenate([mass[pl.ds(r, L, stride=R), :] for r in range(R)], axis=0)
    mass_hi, mass_lo = halves(by_row)
    mass_at = jnp.dot(mass_hi, onehot[...], preferred_element_type=F32) + jnp.dot(
        mass_lo, onehot[...], preferred_element_type=F32
    )
    for v in range(6):
        total = jnp.zeros((L, C), F32)
        for r in range(R):
            total += jnp.where(
                live_rows[v] == r, mass_at[r * L : (r + 1) * L, v * C : (v + 1) * C], 0.0
            )
        turned = left(total, K)
        cm_send[v] = jnp.where(low, total, pltpu.roll(turned, 4, 0))[0:4, :]
        cm_send[v + 6] = jnp.where(low, turned, pltpu.roll(total, 4, 0))[0:4, :]

    pl.semaphore_wait(barrier, len(partners))

    def remote(src, dst, which, device):
        return pltpu.make_async_remote_copy(
            src_ref=src,
            dst_ref=dst,
            send_sem=send_sem.at[which],
            recv_sem=recv_sem.at[which],
            device_id=device,
            device_id_type=MESH,
        )

    far_first = sorted(range(nz), key=lambda i: -min(i, nz - i))
    for i in far_first:
        peer = at_z(i)
        remote(cm_send.at[peer], cm_recv.at[z], MASSES, (other, peer, b)).start()

    halo = [
        remote(send_w, recv_e, EAST, (p, z, west)),
        remote(send_e, recv_w, WEST, (p, z, east)),
        remote(q_hbm.at[:, pl.ds(5, 3), :], field.at[:, pl.ds(5, 3), :], SOUTH, (p, north, b)),
        remote(q_hbm.at[:, pl.ds(0, 3), :], field.at[:, pl.ds(16, 3), :], NORTH, (p, south, b)),
        remote(clat_hbm.at[:, pl.ds(0, 1), :], clat.at[:, pl.ds(R, 1), :], NORTH_C, (p, south, b)),
    ]
    for copy in halo[2:]:
        copy.start()

    loads[0].wait()
    loads[1].wait()
    own = [jnp.zeros((R, C), F32) for _ in range(4)]
    firsts = (0, 4, 124, 120)
    for f in range(F):
        tile = field[f, R : 2 * R, :]
        band = (lane >= 4 * f) & (lane < 4 * f + 4)
        own = [jnp.where(band, left(tile, first - 4 * f), o) for first, o in zip(firsts, own)]
    own_w, own_w2, own_e, own_e2 = own
    edge = [jnp.zeros((R, C), F32) for _ in range(4)]
    firsts = (0, 1, 124, 125)
    for l in range(L):
        tile = clon[l]
        band = (lane >= 4 * l) & (lane < 4 * l + 4)
        edge = [jnp.where(band, left(tile, first - 4 * l), o) for first, o in zip(firsts, edge)]
    edge = [o + pltpu.roll(o, 32, 1) for o in edge]
    c_w, c_w_next, c_e, c_e_next = [o + pltpu.roll(o, 64, 1) for o in edge]
    send_w[0] = own_w
    send_w[1] = c_w
    send_e[0] = own_e
    for copy in halo[:2]:
        copy.start()

    loads[4].wait()
    loads[5].wait()
    cells = slots(lambda d: donor[d])
    start_col = cells & (C - 1)
    start_row = cells >> 7
    row_weights = cubic(slots(lambda d: frac[0, d]))
    col_weights = cubic(slots(lambda d: frac[1, d]))
    for r in range(R):
        roww[r, 0:6, :] = pick(r - start_row, row_weights)
    for v in range(6):
        cols = pl.ds(v * C, C)
        weights = pick(
            column - start_col[v : v + 1, :], [w[v : v + 1, :] for w in col_weights]
        )
        high, low_part = halves(weights)
        colw[0:C, cols] = high
        colw[C : 2 * C, cols] = high
        colw[2 * C : 3 * C, cols] = low_part

    loads[2].wait()
    inside = (lane >= 4) & (lane < 124)
    mass_old = [jnp.zeros((R, C), F32) for _ in range(T)]
    for l in range(L):
        coef = [
            jnp.where(inside, o, 0.0) for o in betas(clon[l], left(clon[l], 1))
        ]
        for t in range(T):
            tile = field[t * L + l, R : 2 * R, :]
            mass_old[t] += mass[l * R : (l + 1) * R, :] * tile
            value = tile
            for k in range(7):
                value -= coef[k] * left(tile, k - 3)
            base[t * L + l] = value

    for copy in halo[:2]:
        copy.wait()
    quarter = lane & 3
    halo_w = jnp.where(b == 0, 0.0, recv_w[0])
    halo_e = jnp.where(b == nlon - 1, 0.0, recv_e[0])
    halo_c = jnp.where(b == nlon - 1, 0.0, recv_e[1])
    c_e_next = jnp.where(quarter == 3, left(halo_c, -3), c_e_next)

    def packed(before, middle, after, coef):
        value = coef[3] * middle
        for k in range(7):
            s = k - 3
            if s < 0:
                cell = jnp.where(quarter < -s, left(before, 4 + s), left(middle, s))
            elif s > 0:
                cell = jnp.where(quarter >= 4 - s, left(after, s - 4), left(middle, s))
            else:
                continue
            value += coef[k] * cell
        return value

    change_w = packed(halo_w, own_w, own_w2, betas(c_w, c_w_next))
    change_e = packed(own_e2, own_e, halo_e, betas(c_e, c_e_next))

    for copy in halo[2:]:
        copy.wait()

    @pl.when(z == 0)
    def _():
        field[:, 5:8, :] = jnp.zeros((F, 3, C), F32)

    @pl.when(z == nz - 1)
    def _():
        field[:, 16:19, :] = jnp.zeros((F, 3, C), F32)
        clat[:, 8:9, :] = jnp.zeros((L, 1, C), F32)

    keep = filled < 0.5
    mass_new = [jnp.zeros((R, C), F32) for _ in range(T)]
    for l in range(L):
        coef = betas(clat[l, 0:8, :], clat[l, 1:9, :])
        kept = jnp.where(keep, mass[l * R : (l + 1) * R, :], 0.0)
        for t in range(T):
            f = t * L + l
            value = base[f]
            value -= jnp.where(lane < 4, left(change_w, 4 * f), 0.0)
            value -= jnp.where(lane >= 124, left(change_e, 4 * f + 4), 0.0)
            for k in range(7):
                value -= coef[k] * field[f, 5 + k : 13 + k, :]
            adv[f * R : (f + 1) * R, :] = value
            mass_new[t] += kept * value

    for r in range(R):
        high, low_part = halves(adv[pl.ds(r, F, stride=R), :])
        at = pl.ds(r * F, F)
        lhs[at, 0:C] = high
        lhs[at, C : 2 * C] = low_part
        lhs[at, 2 * C : 3 * C] = high
    mixed[...] = jnp.dot(lhs[...], colw[...], preferred_element_type=F32)
    for v in range(6):
        total = jnp.zeros((F, C), F32)
        for r in range(R):
            total += roww[r, v : v + 1, :] * mixed[r * F : (r + 1) * F, v * C : (v + 1) * C]
        first, second = total[0 : F // 2, :], total[F // 2 : F, :]
        packet[v] = jnp.where(low16, first, left(second, K))
        packet[v + 6] = jnp.where(low16, left(first, K), second)
    for i in far_first:
        peer = at_z(i)
        remote(packet.at[peer], arrived.at[z], MARGIN, (other, peer, b)).start()

    wait_all(cm_recv, recv_sem.at[MASSES])
    parts = [jnp.zeros((R, C), F32) for _ in range(2)]
    for d in range(12):
        four = cm_recv[d]
        eight = jnp.concatenate([four, left(four, K)], axis=0)
        eight = jnp.where(low, eight, left(eight, K))
        for half in range(2):
            parts[half] += eight * packet[d, half * R : (half + 1) * R, :]
    for half in range(2):
        mass_new[half] += jnp.where(low, parts[half], 0.0)
        mass_new[half + 2] += jnp.where(low, 0.0, parts[half])
    stacked = jnp.concatenate(
        [jnp.sum(m, axis=0, keepdims=True) for m in mass_old + mass_new], axis=0
    )
    sums = jnp.sum(stacked, axis=1, keepdims=True)
    row = jnp.sum(jnp.where(lane == sub[0:R, :], sums, 0.0), axis=0, keepdims=True)

    rows[0] = row
    group = [(other, z, b)]
    group += [(core, z, at_x(i)) for i in range(1, NX) for core in (p, other)]
    for i, device in enumerate(group):
        remote(rows.at[0], sum_x.at[i], SUM_X, device).start()
    wait_all(sum_x, recv_sem.at[SUM_X])
    row = row + jnp.sum(sum_x[...], axis=0)
    rows[1] = row
    for i in range(1, ny):
        remote(rows.at[1], sum_y.at[i - 1], SUM_Y, (p, z, at_y(i))).start()
    wait_all(sum_y, recv_sem.at[SUM_Y])
    row = row + jnp.sum(sum_y[...], axis=0)
    rows[2] = row
    for i in range(1, nz):
        remote(rows.at[2], sum_z.at[i - 1], SUM_Z, (p, at_z(i), b)).start()

    wait_all(arrived, recv_sem.at[MARGIN])
    for v in range(6):
        cols = pl.ds(v * C, C)
        one, two = arrived[v], arrived[v + 6]
        first = jnp.where(low16, one, left(two, K))
        second = jnp.where(low16, left(one, K), two)
        values = jnp.concatenate([first, second], axis=0)
        high = values.astype(BF16).astype(F32)
        low_part = values - high
        for r in range(R):
            at = pl.ds(r * F, F)
            here = live_rows[v] == r
            scat_hi[at, cols] = jnp.where(here, high, 0.0).astype(BF16)
            scat_lo[at, cols] = jnp.where(here, low_part, 0.0).astype(BF16)
    nt = (((1,), (1,)), ((), ()))
    scattered[...] = lax.dot_general(
        scat_hi[...], onehot[...], nt, preferred_element_type=F32
    ) + lax.dot_general(scat_lo[...], onehot[...], nt, preferred_element_type=F32)
    for f in range(F):
        at = pl.ds(f * R, R)
        out[f] = jnp.where(keep, adv[at, :], scattered[pl.ds(f, R, stride=F), :])

    wait_all(sum_z, recv_sem.at[SUM_Z])
    row = row + jnp.sum(sum_z[...], axis=0)
    ratio = row / left(row, 4)
    for t in range(T):
        scale_out[t] = jnp.broadcast_to(ratio[:, t : t + 1], (R, C))

    wait_all(cm_send, send_sem.at[MASSES])
    wait_all(packet, send_sem.at[MARGIN])
    wait_all(sum_x, send_sem.at[SUM_X])
    wait_all(sum_y, send_sem.at[SUM_Y])
    wait_all(sum_z, send_sem.at[SUM_Z])


def solution(mesh):
    nz, nlon = mesh.shape["lat"], mesh.shape["lon"]
    ny = nlon // NX

    def body(tracers, courant_lon, courant_lat, cell_mass, donor_cell, donor_frac, target_cell, live_count):
        slots = nz * K
        hbm_spec = pl.BlockSpec(memory_space=pltpu.HBM)
        vmem_spec = pl.BlockSpec(memory_space=pltpu.VMEM)

        def run(*refs):
            kernel(nz, nlon, *refs)

        merged, scale = pl.pallas_call(
            run,
            out_shape=(
                pltpu.VMEM((F, R, C), F32),
                pltpu.VMEM((T, R, C), F32),
            ),
            in_specs=[hbm_spec] * 8,
            out_specs=(vmem_spec, vmem_spec),
            scratch_shapes=[
                pltpu.VMEM((F, 3 * R, C), F32),
                pltpu.VMEM((L, R, C), F32),
                pltpu.VMEM((L, 2 * R, C), F32),
                pltpu.VMEM((L * R, C), F32),
                pltpu.VMEM((nz, 1, K), jnp.int32),
                pltpu.VMEM((2, nz, 1, K), F32),
                pltpu.VMEM((nz, 1, K), jnp.int32),
                pltpu.SMEM((nz,), jnp.int32),
                pltpu.VMEM((2, R, C), F32),
                pltpu.VMEM((1, R, C), F32),
                pltpu.VMEM((1, R, C), F32),
                pltpu.VMEM((2, R, C), F32),
                pltpu.VMEM((nz, 4, C), F32),
                pltpu.VMEM((nz, 4, C), F32),
                pltpu.VMEM((nz, 2 * R, C), F32),
                pltpu.VMEM((nz, 2 * R, C), F32),
                pltpu.VMEM((3, 1, C), F32),
                pltpu.VMEM((2 * NX - 1, 1, C), F32),
                pltpu.VMEM((ny - 1, 1, C), F32),
                pltpu.VMEM((nz - 1, 1, C), F32),
                pltpu.VMEM((F, R, C), F32),
                pltpu.VMEM((F * R, C), F32),
                pltpu.VMEM((C, slots), BF16),
                pltpu.VMEM((3 * C, slots), BF16),
                pltpu.VMEM((R, R, C), F32),
                pltpu.VMEM((F * R, 3 * C), BF16),
                pltpu.VMEM((F * R, slots), F32),
                pltpu.VMEM((F * R, slots), BF16),
                pltpu.VMEM((F * R, slots), BF16),
                pltpu.VMEM((2 * R, slots), BF16),
                pltpu.VMEM((F * R, C), F32),
                pltpu.SemaphoreType.DMA((8,)),
                pltpu.SemaphoreType.DMA((10,)),
                pltpu.SemaphoreType.DMA((10,)),
            ],
            compiler_params=pltpu.CompilerParams(collective_id=0, has_side_effects=True),
        )(
            tracers.reshape(F, R, C),
            courant_lon.reshape(L, R, C),
            courant_lat.reshape(L, R, C),
            cell_mass.reshape(L * R, C),
            donor_cell.reshape(nz, 1, K),
            donor_frac.reshape(2, nz, 1, K),
            target_cell.reshape(nz, 1, K),
            live_count.reshape(nz),
        )
        return merged.reshape(1, T, L, R, C) * scale.reshape(1, T, 1, R, C)

    lon = "lon"
    placed = (
        P("panel", None, None, "lat", lon),
        P("panel", None, "lat", lon),
        P("panel", None, "lat", lon),
        P("panel", None, "lat", lon),
        P("panel", "lat", lon, None, None),
        P(None, "panel", "lat", lon, None, None),
        P("panel", "lat", lon, None, None),
        P("panel", "lat", lon, None),
    )
    return jax.shard_map(
        body,
        mesh=mesh,
        in_specs=placed,
        out_specs=P("panel", None, None, "lat", lon),
        check_vma=False,
    )
```

```python
import jax
import jax.numpy as jnp
from jax import lax
from jax.experimental import pallas as pl
from jax.experimental.pallas import tpu as pltpu
from jax.sharding import PartitionSpec as P

F32 = jnp.float32
BF16 = jnp.bfloat16
MESH = pl.DeviceIdType.MESH

T = 4
L = 8
F = T * L
R = 8
C = 128
K = 64
NX = 4
WEST, EAST, SOUTH, NORTH, NORTH_C, MASSES, MARGIN, SUM_XY, SUM_Z = range(9)


def left(x, by):
    by = by % C
    return x if by == 0 else pltpu.roll(x, (C - by) % C, x.ndim - 1)


def alphas(c):
    s = jnp.abs(c)
    m = 0.5 * s
    n = m - m * s * (2.0 / 3.0)
    n3 = 3.0 * n
    k1 = c * (1.0 - m - n3)
    k0 = c * (m - n3)
    ka = 2.0 * n3 * c
    u = k0 * (1.0 / 12.0)
    w = k1 * (1.0 / 12.0)
    pos = c > 0.0
    zero = jnp.zeros_like(c)
    near = 7.0 * (u + w) + ka
    far = 7.0 * u - w
    mid = 7.0 * w - u
    return (
        jnp.where(pos, -u, zero),
        jnp.where(pos, far, -w),
        jnp.where(pos, near, mid),
        jnp.where(pos, mid, near),
        jnp.where(pos, -w, far),
        jnp.where(pos, zero, -u),
    )


def betas(c, c_next):
    here, after = alphas(c), alphas(c_next)
    return [-here[0]] + [after[k - 1] - here[k] for k in range(1, 6)] + [after[5]]


def cubic(t):
    a, b, d = t + 1.0, t - 1.0, t - 2.0
    return (
        -t * b * d * (1.0 / 6.0),
        a * b * d * 0.5,
        -a * t * d * 0.5,
        a * t * b * (1.0 / 6.0),
    )


def pick(delta, weights):
    value = jnp.where(delta == 0, weights[0], 0.0)
    for i in range(1, 4):
        value = jnp.where(delta == i, weights[i], value)
    return value


def halves(x):
    high = x.astype(BF16)
    return high, (x - high.astype(F32)).astype(BF16)


def wait_all(ref, sem):
    pltpu.make_async_copy(ref, ref, sem).wait()


def kernel(nz, nlon, q_hbm, clon_hbm, clat_hbm, mass_hbm, donor_hbm, frac_hbm, target_hbm, live_hbm,
           out, scale_out, field, clon, clat, mass, donor, frac, target, live, send_w, send_e, recv_w, recv_e,
           cm_send, cm_recv, relayed, packet, arrived, rows, sum_xy, sum_z, base, adv, onehot, colw,
           roww, lhs, mixed, scat_hi, scat_lo, rowmask, scattered, local_sem, send_sem, recv_sem, relay_send, relay_recv, plane_sem):
    p = lax.axis_index("panel")
    z = lax.axis_index("lat")
    b = lax.axis_index("lon")
    x, y = lax.rem(b, NX), lax.div(b, NX)
    ny = nlon // NX
    other = 1 - p

    def at_z(step):
        return lax.rem(z + step, nz)

    west, east = lax.rem(b + nlon - 1, nlon), lax.rem(b + 1, nlon)
    south, north = at_z(nz - 1), at_z(1)

    loads = [
        pltpu.make_async_copy(q_hbm, field.at[:, pl.ds(R, R), :], local_sem.at[0]),
        pltpu.make_async_copy(clon_hbm, clon, local_sem.at[1]),
        pltpu.make_async_copy(clat_hbm, clat.at[:, pl.ds(0, R), :], local_sem.at[2]),
        pltpu.make_async_copy(mass_hbm, mass, local_sem.at[3]),
        pltpu.make_async_copy(donor_hbm, donor, local_sem.at[4]),
        pltpu.make_async_copy(frac_hbm, frac, local_sem.at[5]),
        pltpu.make_async_copy(target_hbm, target, local_sem.at[6]),
        pltpu.make_async_copy(live_hbm, live, local_sem.at[7]),
    ]
    barrier = pltpu.get_barrier_semaphore()
    far_first = sorted(range(nz), key=lambda i: -min(i, nz - i))
    plane = [(i, j) for i in range(ny) for j in range(NX) if i + j > 0]
    plane.sort(key=lambda ij: -min(ij[0], ny - ij[0]) - min(ij[1], NX - ij[1]))

    def at_plane(i, j):
        return lax.rem(y + i, ny) * NX + lax.rem(x + j, NX)

    def signal(sem, device):
        pl.semaphore_signal(sem, inc=1, device_id=device, device_id_type=MESH)

    far = sorted(range(4, nz - 3), key=lambda i: -min(i, nz - i))
    far_low = min(far)
    close = [i for i in far_first if i not in far]
    across = [at_plane(0, j) for j in range(1, NX)]
    along = [at_plane(2, 0), at_plane(ny - 2, 0)]
    greeted = [(core, at_z(i), b) for i in close if i for core in (other, p)] + [(other, z, b)]
    greeted += [(p, z, c) for c in along + across + [at_plane(1, 0), at_plane(ny - 1, 0), west, east]]
    lower = sum(lax.div(z + i, nz) for i in far)

    for load in (loads[6], loads[7], loads[3], *loads[:3], *loads[4:6]):
        load.start()
    for i in far:

        @pl.when(z + i < nz)
        def _():
            for core in (other, p):
                signal(barrier, (core, z + i, b))

    for device in greeted:
        signal(barrier, device)

    lane = lax.broadcasted_iota(jnp.int32, (R, C), 1)
    lane16 = lax.broadcasted_iota(jnp.int32, (2 * R, C), 1)
    lane_row = lax.broadcasted_iota(jnp.int32, (1, C), 1)
    sub = lax.broadcasted_iota(jnp.int32, (2 * R, C), 0)
    column = lax.broadcasted_iota(jnp.int32, (C, C), 0)
    low, low16 = lane < K, lane16 < K

    loads[6].wait()
    loads[7].wait()

    def slots(read):
        return jnp.concatenate(
            [jnp.concatenate([read(v), read(v + 6)], axis=1) for v in range(6)], axis=0
        )

    spots = slots(lambda d: target[d])
    spot_col = spots & (C - 1)
    spot_row = spots >> 7
    live_rows = []
    for v in range(6):
        count = jnp.where(lane_row < K, live[v], live[v + 6])
        live_rows.append(jnp.where((lane_row & (K - 1)) < count, spot_row[v : v + 1, :], R))
    for v in range(6):
        cols = pl.ds(v * C, C)
        onehot[:, cols] = jnp.where(column == spot_col[v : v + 1, :], 1.0, 0.0).astype(BF16)
        rowmask[:, cols] = jnp.where(sub == live_rows[v], 1.0, 0.0).astype(BF16)
    filled = lax.dot_general(
        rowmask[...], onehot[...], (((1,), (1,)), ((), ())), preferred_element_type=F32
    )[0:R, :]

    loads[3].wait()
    by_row = jnp.concatenate([mass[pl.ds(r, L, stride=R), :] for r in range(R)], axis=0)
    mass_hi, mass_lo = halves(by_row)
    mass_at = jnp.dot(mass_hi, onehot[...], preferred_element_type=F32) + jnp.dot(
        mass_lo, onehot[...], preferred_element_type=F32
    )
    for v in range(6):
        total = jnp.zeros((L, C), F32)
        for r in range(R):
            total += jnp.where(
                live_rows[v] == r, mass_at[r * L : (r + 1) * L, v * C : (v + 1) * C], 0.0
            )
        turned = left(total, K)
        cm_send[v] = jnp.where(low, total, pltpu.roll(turned, 4, 0))[0:4, :]
        cm_send[v + 6] = jnp.where(low, turned, pltpu.roll(total, 4, 0))[0:4, :]

    pl.semaphore_wait(barrier, len(greeted) + 2 * lower)

    def remote(src, dst, which, device):
        return pltpu.make_async_remote_copy(
            src_ref=src,
            dst_ref=dst,
            send_sem=send_sem.at[which],
            recv_sem=recv_sem.at[which],
            device_id=device,
            device_id_type=MESH,
        )

    def send_masses(peer):
        remote(cm_send.at[peer], cm_recv.at[z], MASSES, (other, peer, b)).start()

    def relay(src, dst, i, device):
        return pltpu.make_async_remote_copy(
            src_ref=src,
            dst_ref=dst,
            send_sem=relay_send.at[i - far_low],
            recv_sem=relay_recv.at[i - far_low],
            device_id=device,
            device_id_type=MESH,
        )

    def relay_step(i):
        return 3 if 2 * i <= nz else nz - 3

    for i in far:

        @pl.when(z + i >= nz)
        def _():
            send_masses(z + i - nz)

        @pl.when(z + i < nz)
        def _():
            via = (other, at_z(relay_step(i)), b)
            relay(cm_send.at[z + i], relayed.at[i - far_low], i, via).start()

    for i in close:
        send_masses(at_z(i))

    halo = [
        remote(send_w, recv_e, EAST, (p, z, west)),
        remote(send_e, recv_w, WEST, (p, z, east)),
        remote(q_hbm.at[:, pl.ds(5, 3), :], field.at[:, pl.ds(5, 3), :], SOUTH, (p, north, b)),
        remote(q_hbm.at[:, pl.ds(0, 3), :], field.at[:, pl.ds(16, 3), :], NORTH, (p, south, b)),
        remote(clat_hbm.at[:, pl.ds(0, 1), :], clat.at[:, pl.ds(R, 1), :], NORTH_C, (p, south, b)),
    ]
    for copy in halo[2:]:
        copy.start()

    loads[0].wait()
    loads[1].wait()
    own = [jnp.zeros((R, C), F32) for _ in range(4)]
    firsts = (0, 4, 124, 120)
    for f in range(F):
        tile = field[f, R : 2 * R, :]
        band = (lane >= 4 * f) & (lane < 4 * f + 4)
        own = [jnp.where(band, left(tile, first - 4 * f), o) for first, o in zip(firsts, own)]
    own_w, own_w2, own_e, own_e2 = own
    edge = [jnp.zeros((R, C), F32) for _ in range(4)]
    firsts = (0, 1, 124, 125)
    for l in range(L):
        tile = clon[l]
        band = (lane >= 4 * l) & (lane < 4 * l + 4)
        edge = [jnp.where(band, left(tile, first - 4 * l), o) for first, o in zip(firsts, edge)]
    edge = [o + pltpu.roll(o, 32, 1) for o in edge]
    c_w, c_w_next, c_e, c_e_next = [o + pltpu.roll(o, 64, 1) for o in edge]
    send_w[0] = own_w
    send_w[1] = c_w
    send_e[0] = own_e
    for copy in halo[:2]:
        copy.start()
    for c in along:
        signal(plane_sem.at[0], (p, z, c))

    loads[4].wait()
    loads[5].wait()
    cells = slots(lambda d: donor[d])
    start_col = cells & (C - 1)
    start_row = cells >> 7
    row_weights = cubic(slots(lambda d: frac[0, d]))
    col_weights = cubic(slots(lambda d: frac[1, d]))
    for r in range(R):
        roww[r, 0:6, :] = pick(r - start_row, row_weights)
    for v in range(6):
        cols = pl.ds(v * C, C)
        weights = pick(
            column - start_col[v : v + 1, :], [w[v : v + 1, :] for w in col_weights]
        )
        high, low_part = halves(weights)
        colw[0:C, cols] = high
        colw[C : 2 * C, cols] = high
        colw[2 * C : 3 * C, cols] = low_part

    loads[2].wait()
    inside = (lane >= 4) & (lane < 124)
    mass_old = [jnp.zeros((R, C), F32) for _ in range(T)]
    for l in range(L):
        coef = [
            jnp.where(inside, o, 0.0) for o in betas(clon[l], left(clon[l], 1))
        ]
        for t in range(T):
            tile = field[t * L + l, R : 2 * R, :]
            mass_old[t] += mass[l * R : (l + 1) * R, :] * tile
            value = tile
            for k in range(7):
                value -= coef[k] * left(tile, k - 3)
            base[t * L + l] = value

    pl.semaphore_wait(plane_sem.at[0], 2)
    for c in across:
        signal(plane_sem.at[1], (p, z, c))
    for i in far:
        origin = at_z(nz - relay_step(i))

        @pl.when(origin + i < nz)
        def _():
            slot = relayed.at[i - far_low]
            pltpu.make_async_copy(slot, slot, relay_recv.at[i - far_low]).wait()
            remote(slot, cm_recv.at[origin], MASSES, (p, origin + i, b)).start()

    for copy in halo[:2]:
        copy.wait()
    quarter = lane & 3
    halo_w = jnp.where(b == 0, 0.0, recv_w[0])
    halo_e = jnp.where(b == nlon - 1, 0.0, recv_e[0])
    halo_c = jnp.where(b == nlon - 1, 0.0, recv_e[1])
    c_e_next = jnp.where(quarter == 3, left(halo_c, -3), c_e_next)

    def packed(before, middle, after, coef):
        value = coef[3] * middle
        for k in range(7):
            s = k - 3
            if s < 0:
                cell = jnp.where(quarter < -s, left(before, 4 + s), left(middle, s))
            elif s > 0:
                cell = jnp.where(quarter >= 4 - s, left(after, s - 4), left(middle, s))
            else:
                continue
            value += coef[k] * cell
        return value

    change_w = packed(halo_w, own_w, own_w2, betas(c_w, c_w_next))
    change_e = packed(own_e2, own_e, halo_e, betas(c_e, c_e_next))

    for copy in halo[2:]:
        copy.wait()

    @pl.when(z == 0)
    def _():
        field[:, 5:8, :] = jnp.zeros((F, 3, C), F32)

    @pl.when(z == nz - 1)
    def _():
        field[:, 16:19, :] = jnp.zeros((F, 3, C), F32)
        clat[:, 8:9, :] = jnp.zeros((L, 1, C), F32)

    keep = filled < 0.5
    mass_new = [jnp.zeros((R, C), F32) for _ in range(T)]
    for l in range(L):
        coef = betas(clat[l, 0:8, :], clat[l, 1:9, :])
        kept = jnp.where(keep, mass[l * R : (l + 1) * R, :], 0.0)
        for t in range(T):
            f = t * L + l
            value = base[f]
            value -= jnp.where(lane < 4, left(change_w, 4 * f), 0.0)
            value -= jnp.where(lane >= 124, left(change_e, 4 * f + 4), 0.0)
            for k in range(7):
                value -= coef[k] * field[f, 5 + k : 13 + k, :]
            adv[f * R : (f + 1) * R, :] = value
            mass_new[t] += kept * value

    for r in range(R):
        high, low_part = halves(adv[pl.ds(r, F, stride=R), :])
        at = pl.ds(r * F, F)
        lhs[at, 0:C] = high
        lhs[at, C : 2 * C] = low_part
        lhs[at, 2 * C : 3 * C] = high
    mixed[...] = jnp.dot(lhs[...], colw[...], preferred_element_type=F32)
    for v in range(6):
        total = jnp.zeros((F, C), F32)
        for r in range(R):
            total += roww[r, v : v + 1, :] * mixed[r * F : (r + 1) * F, v * C : (v + 1) * C]
        first, second = total[0 : F // 2, :], total[F // 2 : F, :]
        packet[v] = jnp.where(low16, first, left(second, K))
        packet[v + 6] = jnp.where(low16, left(first, K), second)

    wait_all(cm_recv, recv_sem.at[MASSES])
    for i in far_first:
        peer = at_z(i)
        remote(packet.at[peer], arrived.at[z], MARGIN, (other, peer, b)).start()
    parts = [jnp.zeros((R, C), F32) for _ in range(2)]
    for d in range(12):
        four = cm_recv[d]
        eight = jnp.concatenate([four, left(four, K)], axis=0)
        eight = jnp.where(low, eight, left(eight, K))
        for half in range(2):
            parts[half] += eight * packet[d, half * R : (half + 1) * R, :]
    for half in range(2):
        mass_new[half] += jnp.where(low, parts[half], 0.0)
        mass_new[half + 2] += jnp.where(low, 0.0, parts[half])
    stacked = jnp.concatenate(
        [jnp.sum(m, axis=0, keepdims=True) for m in mass_old + mass_new], axis=0
    )
    sums = jnp.sum(stacked, axis=1, keepdims=True)
    row = jnp.sum(jnp.where(lane == sub[0:R, :], sums, 0.0), axis=0, keepdims=True)

    rows[0:1, :] = row
    pl.semaphore_wait(plane_sem.at[1], len(across))
    for n, (i, j) in enumerate(plane):
        remote(rows.at[pl.ds(0, 1), :], sum_xy.at[pl.ds(n, 1), :], SUM_XY, (p, z, at_plane(i, j))).start()
    wait_all(sum_xy, recv_sem.at[SUM_XY])
    row = row + jnp.sum(sum_xy[...], axis=0, keepdims=True)
    rows[1:2, :] = row
    line = [(core, i) for i in far_first if i > 0 for core in (p, other)] + [(other, 0)]
    for n, (core, i) in enumerate(line):
        remote(rows.at[pl.ds(1, 1), :], sum_z.at[pl.ds(n, 1), :], SUM_Z, (core, at_z(i), b)).start()

    wait_all(arrived, recv_sem.at[MARGIN])
    for v in range(6):
        cols = pl.ds(v * C, C)
        one, two = arrived[v], arrived[v + 6]
        first = jnp.where(low16, one, left(two, K))
        second = jnp.where(low16, left(one, K), two)
        values = jnp.concatenate([first, second], axis=0)
        high = values.astype(BF16).astype(F32)
        low_part = values - high
        for r in range(R):
            at = pl.ds(r * F, F)
            here = live_rows[v] == r
            scat_hi[at, cols] = jnp.where(here, high, 0.0).astype(BF16)
            scat_lo[at, cols] = jnp.where(here, low_part, 0.0).astype(BF16)
    nt = (((1,), (1,)), ((), ()))
    scattered[...] = lax.dot_general(
        scat_hi[...], onehot[...], nt, preferred_element_type=F32
    ) + lax.dot_general(scat_lo[...], onehot[...], nt, preferred_element_type=F32)
    for f in range(F):
        at = pl.ds(f * R, R)
        out[f] = jnp.where(keep, adv[at, :], scattered[pl.ds(f, R, stride=F), :])

    wait_all(sum_z, recv_sem.at[SUM_Z])
    row = row + jnp.sum(sum_z[...], axis=0, keepdims=True)
    ratio = row / left(row, 4)
    for t in range(T):
        scale_out[t] = jnp.broadcast_to(ratio[:, t : t + 1], (R, C))

    for i in close:
        wait_all(cm_send.at[0], send_sem.at[MASSES])
    for i in far:

        @pl.when(z + i >= nz)
        def _():
            wait_all(cm_send.at[0], send_sem.at[MASSES])

        @pl.when(z + i < nz)
        def _():
            wait_all(cm_send.at[0], relay_send.at[i - far_low])

        @pl.when(at_z(nz - relay_step(i)) + i < nz)
        def _():
            wait_all(cm_send.at[0], send_sem.at[MASSES])

    wait_all(packet, send_sem.at[MARGIN])
    wait_all(sum_xy, send_sem.at[SUM_XY])
    wait_all(sum_z, send_sem.at[SUM_Z])


def solution(mesh):
    nz, nlon = mesh.shape["lat"], mesh.shape["lon"]
    ny = nlon // NX

    def body(tracers, courant_lon, courant_lat, cell_mass, donor_cell, donor_frac, target_cell, live_count):
        slots = nz * K
        hbm_spec = pl.BlockSpec(memory_space=pltpu.HBM)
        vmem_spec = pl.BlockSpec(memory_space=pltpu.VMEM)

        def run(*refs):
            kernel(nz, nlon, *refs)

        merged, scale = pl.pallas_call(
            run,
            out_shape=(
                pltpu.VMEM((F, R, C), F32),
                pltpu.VMEM((T, R, C), F32),
            ),
            in_specs=[hbm_spec] * 8,
            out_specs=(vmem_spec, vmem_spec),
            scratch_shapes=[
                pltpu.VMEM((F, 3 * R, C), F32),
                pltpu.VMEM((L, R, C), F32),
                pltpu.VMEM((L, 2 * R, C), F32),
                pltpu.VMEM((L * R, C), F32),
                pltpu.VMEM((nz, 1, K), jnp.int32),
                pltpu.VMEM((2, nz, 1, K), F32),
                pltpu.VMEM((nz, 1, K), jnp.int32),
                pltpu.SMEM((nz,), jnp.int32),
                pltpu.VMEM((2, R, C), F32),
                pltpu.VMEM((1, R, C), F32),
                pltpu.VMEM((1, R, C), F32),
                pltpu.VMEM((2, R, C), F32),
                pltpu.VMEM((nz, 4, C), F32),
                pltpu.VMEM((nz, 4, C), F32),
                pltpu.VMEM((nz - 7, 4, C), F32),
                pltpu.VMEM((nz, 2 * R, C), F32),
                pltpu.VMEM((nz, 2 * R, C), F32),
                pltpu.VMEM((2, C), F32),
                pltpu.VMEM((nlon - 1, C), F32),
                pltpu.VMEM((2 * nz - 1, C), F32),
                pltpu.VMEM((F, R, C), F32),
                pltpu.VMEM((F * R, C), F32),
                pltpu.VMEM((C, slots), BF16),
                pltpu.VMEM((3 * C, slots), BF16),
                pltpu.VMEM((R, R, C), F32),
                pltpu.VMEM((F * R, 3 * C), BF16),
                pltpu.VMEM((F * R, slots), F32),
                pltpu.VMEM((F * R, slots), BF16),
                pltpu.VMEM((F * R, slots), BF16),
                pltpu.VMEM((2 * R, slots), BF16),
                pltpu.VMEM((F * R, C), F32),
                pltpu.SemaphoreType.DMA((8,)),
                pltpu.SemaphoreType.DMA((9,)),
                pltpu.SemaphoreType.DMA((9,)),
                pltpu.SemaphoreType.DMA((nz - 7,)),
                pltpu.SemaphoreType.DMA((nz - 7,)),
                pltpu.SemaphoreType.REGULAR((2,)),
            ],
            compiler_params=pltpu.CompilerParams(collective_id=0, has_side_effects=True),
        )(
            tracers.reshape(F, R, C),
            courant_lon.reshape(L, R, C),
            courant_lat.reshape(L, R, C),
            cell_mass.reshape(L * R, C),
            donor_cell.reshape(nz, 1, K),
            donor_frac.reshape(2, nz, 1, K),
            target_cell.reshape(nz, 1, K),
            live_count.reshape(nz),
        )
        return merged.reshape(1, T, L, R, C) * scale.reshape(1, T, 1, R, C)

    lon = "lon"
    placed = (
        P("panel", None, None, "lat", lon),
        P("panel", None, "lat", lon),
        P("panel", None, "lat", lon),
        P("panel", None, "lat", lon),
        P("panel", "lat", lon, None, None),
        P(None, "panel", "lat", lon, None, None),
        P("panel", "lat", lon, None, None),
        P("panel", "lat", lon, None),
    )
    return jax.shard_map(
        body,
        mesh=mesh,
        in_specs=placed,
        out_specs=P("panel", None, None, "lat", lon),
        check_vma=False,
    )
```

```python
import jax
import jax.numpy as jnp
from jax import lax
from jax.experimental import pallas as pl
from jax.experimental.pallas import tpu as pltpu
from jax.sharding import PartitionSpec as P

F32 = jnp.float32
BF16 = jnp.bfloat16
MESH = pl.DeviceIdType.MESH

T = 4
L = 8
F = T * L
R = 8
C = 128
K = 64
NX = 4
WEST, EAST, SOUTH, NORTH, NORTH_C, MASSES, MARGIN, SUM_XY, SUM_Z = range(9)


def left(x, by):
    by = by % C
    return x if by == 0 else pltpu.roll(x, (C - by) % C, x.ndim - 1)


def alphas(c):
    s = jnp.abs(c)
    m = 0.5 * s
    n = m - m * s * (2.0 / 3.0)
    n3 = 3.0 * n
    k1 = c * (1.0 - m - n3)
    k0 = c * (m - n3)
    ka = 2.0 * n3 * c
    u = k0 * (1.0 / 12.0)
    w = k1 * (1.0 / 12.0)
    pos = c > 0.0
    zero = jnp.zeros_like(c)
    near = 7.0 * (u + w) + ka
    far = 7.0 * u - w
    mid = 7.0 * w - u
    return (
        jnp.where(pos, -u, zero),
        jnp.where(pos, far, -w),
        jnp.where(pos, near, mid),
        jnp.where(pos, mid, near),
        jnp.where(pos, -w, far),
        jnp.where(pos, zero, -u),
    )


def betas(c, c_next):
    here, after = alphas(c), alphas(c_next)
    return [-here[0]] + [after[k - 1] - here[k] for k in range(1, 6)] + [after[5]]


def cubic(t):
    a, b, d = t + 1.0, t - 1.0, t - 2.0
    return (
        -t * b * d * (1.0 / 6.0),
        a * b * d * 0.5,
        -a * t * d * 0.5,
        a * t * b * (1.0 / 6.0),
    )


def pick(delta, weights):
    value = jnp.where(delta == 0, weights[0], 0.0)
    for i in range(1, 4):
        value = jnp.where(delta == i, weights[i], value)
    return value


def halves(x):
    high = x.astype(BF16)
    return high, (x - high.astype(F32)).astype(BF16)


def wait_all(ref, sem):
    pltpu.make_async_copy(ref, ref, sem).wait()


def kernel(nz, nlon, q_hbm, clon_hbm, clat_hbm, mass_hbm, donor_hbm, frac_hbm, target_hbm, live_hbm,
           out, scale_out, field, clon, clat, mass, donor, frac, target, live, send_w, send_e, recv_w, recv_e,
           cm_send, cm_recv, packet, arrived, rows, sum_xy, sum_z, mass_old, base, latw, adv, onehot, colw,
           roww, lhs, mixed, scat_hi, scat_lo, rowmask, scattered, local_sem, send_sem, recv_sem):
    p = lax.axis_index("panel")
    z = lax.axis_index("lat")
    b = lax.axis_index("lon")
    x, y = lax.rem(b, NX), lax.div(b, NX)
    ny = nlon // NX
    other = 1 - p

    def at_z(step):
        return lax.rem(z + step, nz)

    west, east = lax.rem(b + nlon - 1, nlon), lax.rem(b + 1, nlon)
    south, north = at_z(nz - 1), at_z(1)

    loads = [
        pltpu.make_async_copy(q_hbm, field.at[:, pl.ds(R, R), :], local_sem.at[0]),
        pltpu.make_async_copy(clon_hbm, clon, local_sem.at[1]),
        pltpu.make_async_copy(clat_hbm, clat.at[:, pl.ds(0, R), :], local_sem.at[2]),
        pltpu.make_async_copy(mass_hbm, mass, local_sem.at[3]),
        pltpu.make_async_copy(donor_hbm, donor, local_sem.at[4]),
        pltpu.make_async_copy(frac_hbm, frac, local_sem.at[5]),
        pltpu.make_async_copy(target_hbm, target, local_sem.at[6]),
        pltpu.make_async_copy(live_hbm, live, local_sem.at[7]),
    ]
    barrier = pltpu.get_barrier_semaphore()
    far_first = sorted(range(nz), key=lambda i: -min(i, nz - i))
    partners = [(core, at_z(i), b) for i in far_first[:-1] for core in (other, p)] + [(other, z, b)]
    plane = [(i, j) for i in range(ny) for j in range(NX) if i + j > 0]
    plane.sort(key=lambda ij: -min(ij[0], ny - ij[0]) - min(ij[1], NX - ij[1]))

    def at_plane(i, j):
        return lax.rem(y + i, ny) * NX + lax.rem(x + j, NX)

    partners += [(p, z, at_plane(i, j)) for i, j in plane]
    for load in (loads[6], loads[7], loads[3], *loads[:3], *loads[4:6]):
        load.start()
    for partner in partners:
        pl.semaphore_signal(barrier, inc=1, device_id=partner, device_id_type=MESH)

    lane = lax.broadcasted_iota(jnp.int32, (R, C), 1)
    lane16 = lax.broadcasted_iota(jnp.int32, (2 * R, C), 1)
    lane_row = lax.broadcasted_iota(jnp.int32, (1, C), 1)
    sub = lax.broadcasted_iota(jnp.int32, (2 * R, C), 0)
    column = lax.broadcasted_iota(jnp.int32, (C, C), 0)
    low, low16 = lane < K, lane16 < K

    loads[6].wait()
    loads[7].wait()

    def slots(read):
        return jnp.concatenate(
            [jnp.concatenate([read(v), read(v + 6)], axis=1) for v in range(6)], axis=0
        )

    spots = slots(lambda d: target[d])
    spot_col = spots & (C - 1)
    spot_row = spots >> 7
    live_rows = []
    for v in range(6):
        count = jnp.where(lane_row < K, live[v], live[v + 6])
        live_rows.append(jnp.where((lane_row & (K - 1)) < count, spot_row[v : v + 1, :], R))
    for v in range(6):
        cols = pl.ds(v * C, C)
        onehot[:, cols] = jnp.where(column == spot_col[v : v + 1, :], 1.0, 0.0).astype(BF16)
        rowmask[:, cols] = jnp.where(sub == live_rows[v], 1.0, 0.0).astype(BF16)
    filled = lax.dot_general(
        rowmask[...], onehot[...], (((1,), (1,)), ((), ())), preferred_element_type=F32
    )[0:R, :]

    loads[3].wait()
    by_row = jnp.concatenate([mass[pl.ds(r, L, stride=R), :] for r in range(R)], axis=0)
    mass_hi, mass_lo = halves(by_row)
    mass_at = jnp.dot(mass_hi, onehot[...], preferred_element_type=F32) + jnp.dot(
        mass_lo, onehot[...], preferred_element_type=F32
    )
    for v in range(6):
        total = jnp.zeros((L, C), F32)
        for r in range(R):
            total += jnp.where(
                live_rows[v] == r, mass_at[r * L : (r + 1) * L, v * C : (v + 1) * C], 0.0
            )
        turned = left(total, K)
        cm_send[v] = jnp.where(low, total, pltpu.roll(turned, 4, 0))[0:4, :]
        cm_send[v + 6] = jnp.where(low, turned, pltpu.roll(total, 4, 0))[0:4, :]

    loads[0].wait()
    loads[1].wait()
    loads[2].wait()
    own = [jnp.zeros((R, C), F32) for _ in range(4)]
    firsts = (0, 4, 124, 120)
    for f in range(F):
        tile = field[f, R : 2 * R, :]
        band = (lane >= 4 * f) & (lane < 4 * f + 4)
        own = [jnp.where(band, left(tile, first - 4 * f), o) for first, o in zip(firsts, own)]
    own_w, own_w2, own_e, own_e2 = own
    edge = [jnp.zeros((R, C), F32) for _ in range(4)]
    firsts = (0, 1, 124, 125)
    for l in range(L):
        tile = clon[l]
        band = (lane >= 4 * l) & (lane < 4 * l + 4)
        edge = [jnp.where(band, left(tile, first - 4 * l), o) for first, o in zip(firsts, edge)]
    edge = [o + pltpu.roll(o, 32, 1) for o in edge]
    c_w, c_w_next, c_e, c_e_next = [o + pltpu.roll(o, 64, 1) for o in edge]
    send_w[0] = own_w
    send_w[1] = c_w
    send_e[0] = own_e
    def prepare():
        loads[4].wait()
        loads[5].wait()
        cells = slots(lambda d: donor[d])
        start_col = cells & (C - 1)
        start_row = cells >> 7
        row_weights = cubic(slots(lambda d: frac[0, d]))
        col_weights = cubic(slots(lambda d: frac[1, d]))
        for r in range(R):
            roww[r, 0:6, :] = pick(r - start_row, row_weights)
        for v in range(6):
            cols = pl.ds(v * C, C)
            weights = pick(
                column - start_col[v : v + 1, :], [w[v : v + 1, :] for w in col_weights]
            )
            high, low_part = halves(weights)
            colw[0:C, cols] = high
            colw[C : 2 * C, cols] = high
            colw[2 * C : 3 * C, cols] = low_part

        inside = (lane >= 4) & (lane < 124)
        old = [jnp.zeros((R, C), F32) for _ in range(T)]
        for l in range(L):
            coef = [
                jnp.where(inside, o, 0.0) for o in betas(clon[l], left(clon[l], 1))
            ]
            for t in range(T):
                tile = field[t * L + l, R : 2 * R, :]
                old[t] += mass[l * R : (l + 1) * R, :] * tile
                value = tile
                for k in range(7):
                    value -= coef[k] * left(tile, k - 3)
                base[t * L + l] = value
        for t in range(T):
            mass_old[t] = old[t]

    late = z >= nz - 4
    pl.when(jnp.logical_not(late))(prepare)
    pl.semaphore_wait(barrier, len(partners))

    def remote(src, dst, which, device):
        return pltpu.make_async_remote_copy(
            src_ref=src,
            dst_ref=dst,
            send_sem=send_sem.at[which],
            recv_sem=recv_sem.at[which],
            device_id=device,
            device_id_type=MESH,
        )

    far_first = sorted(range(nz), key=lambda i: -min(i, nz - i))
    halo = [
        remote(send_w, recv_e, EAST, (p, z, west)),
        remote(send_e, recv_w, WEST, (p, z, east)),
        remote(field.at[:, pl.ds(13, 3), :], field.at[:, pl.ds(5, 3), :], SOUTH, (p, north, b)),
        remote(field.at[:, pl.ds(8, 3), :], field.at[:, pl.ds(16, 3), :], NORTH, (p, south, b)),
        remote(clat.at[:, pl.ds(0, 1), :], clat.at[:, pl.ds(R, 1), :], NORTH_C, (p, south, b)),
    ]
    for copy in halo[:2]:
        copy.start()
    for i in far_first[:5]:
        peer = at_z(i)
        remote(cm_send.at[peer], cm_recv.at[z], MASSES, (other, peer, b)).start()
    for copy in halo[2:]:
        copy.start()
    for i in far_first[5:]:
        peer = at_z(i)
        remote(cm_send.at[peer], cm_recv.at[z], MASSES, (other, peer, b)).start()

    pl.when(late)(prepare)
    for copy in halo[:2]:
        copy.wait()
    quarter = lane & 3
    halo_w = jnp.where(b == 0, 0.0, recv_w[0])
    halo_e = jnp.where(b == nlon - 1, 0.0, recv_e[0])
    halo_c = jnp.where(b == nlon - 1, 0.0, recv_e[1])
    c_e_next = jnp.where(quarter == 3, left(halo_c, -3), c_e_next)

    def packed(before, middle, after, coef):
        value = coef[3] * middle
        for k in range(7):
            s = k - 3
            if s < 0:
                cell = jnp.where(quarter < -s, left(before, 4 + s), left(middle, s))
            elif s > 0:
                cell = jnp.where(quarter >= 4 - s, left(after, s - 4), left(middle, s))
            else:
                continue
            value += coef[k] * cell
        return value

    change_w = packed(halo_w, own_w, own_w2, betas(c_w, c_w_next))
    change_e = packed(own_e2, own_e, halo_e, betas(c_e, c_e_next))

    for f in range(F):
        value = base[f] - jnp.where(lane < 4, left(change_w, 4 * f), 0.0)
        base[f] = value - jnp.where(lane >= 124, left(change_e, 4 * f + 4), 0.0)

    halo[4].wait()

    @pl.when(z == nz - 1)
    def _():
        clat[:, 8:9, :] = jnp.zeros((L, 1, C), F32)

    for l in range(L):
        for k, coef in enumerate(betas(clat[l, 0:8, :], clat[l, 1:9, :])):
            latw[l, k] = coef

    for copy in halo[2:4]:
        copy.wait()

    @pl.when(z == 0)
    def _():
        field[:, 5:8, :] = jnp.zeros((F, 3, C), F32)

    @pl.when(z == nz - 1)
    def _():
        field[:, 16:19, :] = jnp.zeros((F, 3, C), F32)

    keep = filled < 0.5
    mass_new = [jnp.zeros((R, C), F32) for _ in range(T)]
    for l in range(L):
        coef = [latw[l, k] for k in range(7)]
        kept = jnp.where(keep, mass[l * R : (l + 1) * R, :], 0.0)
        for t in range(T):
            f = t * L + l
            value = base[f]
            for k in range(7):
                value -= coef[k] * field[f, 5 + k : 13 + k, :]
            adv[f * R : (f + 1) * R, :] = value
            mass_new[t] += kept * value

    for r in range(R):
        high, low_part = halves(adv[pl.ds(r, F, stride=R), :])
        at = pl.ds(r * F, F)
        lhs[at, 0:C] = high
        lhs[at, C : 2 * C] = low_part
        lhs[at, 2 * C : 3 * C] = high
    mixed[...] = jnp.dot(lhs[...], colw[...], preferred_element_type=F32)
    for v in range(6):
        total = jnp.zeros((F, C), F32)
        for r in range(R):
            total += roww[r, v : v + 1, :] * mixed[r * F : (r + 1) * F, v * C : (v + 1) * C]
        first, second = total[0 : F // 2, :], total[F // 2 : F, :]
        packet[v] = jnp.where(low16, first, left(second, K))
        packet[v + 6] = jnp.where(low16, left(first, K), second)
    for i in far_first:
        peer = at_z(i)
        remote(packet.at[peer], arrived.at[z], MARGIN, (other, peer, b)).start()

    wait_all(cm_recv, recv_sem.at[MASSES])
    parts = [jnp.zeros((R, C), F32) for _ in range(2)]
    for d in range(12):
        four = cm_recv[d]
        eight = jnp.concatenate([four, left(four, K)], axis=0)
        eight = jnp.where(low, eight, left(eight, K))
        for half in range(2):
            parts[half] += eight * packet[d, half * R : (half + 1) * R, :]
    for half in range(2):
        mass_new[half] += jnp.where(low, parts[half], 0.0)
        mass_new[half + 2] += jnp.where(low, 0.0, parts[half])
    stacked = jnp.concatenate(
        [jnp.sum(m, axis=0, keepdims=True) for m in [mass_old[t] for t in range(T)] + mass_new], axis=0
    )
    sums = jnp.sum(stacked, axis=1, keepdims=True)
    row = jnp.sum(jnp.where(lane == sub[0:R, :], sums, 0.0), axis=0, keepdims=True)

    rows[0:1, :] = row
    for n, (i, j) in enumerate(plane):
        remote(rows.at[pl.ds(0, 1), :], sum_xy.at[pl.ds(n, 1), :], SUM_XY, (p, z, at_plane(i, j))).start()
    wait_all(sum_xy, recv_sem.at[SUM_XY])
    row = row + jnp.sum(sum_xy[...], axis=0, keepdims=True)
    rows[1:2, :] = row
    line = [(core, i) for i in far_first if i > 0 for core in (p, other)] + [(other, 0)]
    for n, (core, i) in enumerate(line):
        remote(rows.at[pl.ds(1, 1), :], sum_z.at[pl.ds(n, 1), :], SUM_Z, (core, at_z(i), b)).start()

    wait_all(arrived, recv_sem.at[MARGIN])
    for v in range(6):
        cols = pl.ds(v * C, C)
        one, two = arrived[v], arrived[v + 6]
        first = jnp.where(low16, one, left(two, K))
        second = jnp.where(low16, left(one, K), two)
        values = jnp.concatenate([first, second], axis=0)
        high = values.astype(BF16).astype(F32)
        low_part = values - high
        for r in range(R):
            at = pl.ds(r * F, F)
            here = live_rows[v] == r
            scat_hi[at, cols] = jnp.where(here, high, 0.0).astype(BF16)
            scat_lo[at, cols] = jnp.where(here, low_part, 0.0).astype(BF16)
    nt = (((1,), (1,)), ((), ()))
    scattered[...] = lax.dot_general(
        scat_hi[...], onehot[...], nt, preferred_element_type=F32
    ) + lax.dot_general(scat_lo[...], onehot[...], nt, preferred_element_type=F32)
    for f in range(F):
        at = pl.ds(f * R, R)
        out[f] = jnp.where(keep, adv[at, :], scattered[pl.ds(f, R, stride=F), :])

    wait_all(sum_z, recv_sem.at[SUM_Z])
    row = row + jnp.sum(sum_z[...], axis=0, keepdims=True)
    ratio = row / left(row, 4)
    for t in range(T):
        scale_out[t] = jnp.broadcast_to(ratio[:, t : t + 1], (R, C))

    wait_all(cm_send, send_sem.at[MASSES])
    wait_all(packet, send_sem.at[MARGIN])
    wait_all(sum_xy, send_sem.at[SUM_XY])
    wait_all(sum_z, send_sem.at[SUM_Z])


def solution(mesh):
    nz, nlon = mesh.shape["lat"], mesh.shape["lon"]
    ny = nlon // NX

    def body(tracers, courant_lon, courant_lat, cell_mass, donor_cell, donor_frac, target_cell, live_count):
        slots = nz * K
        hbm_spec = pl.BlockSpec(memory_space=pltpu.HBM)
        vmem_spec = pl.BlockSpec(memory_space=pltpu.VMEM)

        def run(*refs):
            kernel(nz, nlon, *refs)

        merged, scale = pl.pallas_call(
            run,
            out_shape=(
                pltpu.VMEM((F, R, C), F32),
                pltpu.VMEM((T, R, C), F32),
            ),
            in_specs=[hbm_spec] * 8,
            out_specs=(vmem_spec, vmem_spec),
            scratch_shapes=[
                pltpu.VMEM((F, 3 * R, C), F32),
                pltpu.VMEM((L, R, C), F32),
                pltpu.VMEM((L, 2 * R, C), F32),
                pltpu.VMEM((L * R, C), F32),
                pltpu.VMEM((nz, 1, K), jnp.int32),
                pltpu.VMEM((2, nz, 1, K), F32),
                pltpu.VMEM((nz, 1, K), jnp.int32),
                pltpu.SMEM((nz,), jnp.int32),
                pltpu.VMEM((2, R, C), F32),
                pltpu.VMEM((1, R, C), F32),
                pltpu.VMEM((1, R, C), F32),
                pltpu.VMEM((2, R, C), F32),
                pltpu.VMEM((nz, 4, C), F32),
                pltpu.VMEM((nz, 4, C), F32),
                pltpu.VMEM((nz, 2 * R, C), F32),
                pltpu.VMEM((nz, 2 * R, C), F32),
                pltpu.VMEM((2, C), F32),
                pltpu.VMEM((nlon - 1, C), F32),
                pltpu.VMEM((2 * nz - 1, C), F32),
                pltpu.VMEM((T, R, C), F32),
                pltpu.VMEM((F, R, C), F32),
                pltpu.VMEM((L, 7, R, C), F32),
                pltpu.VMEM((F * R, C), F32),
                pltpu.VMEM((C, slots), BF16),
                pltpu.VMEM((3 * C, slots), BF16),
                pltpu.VMEM((R, R, C), F32),
                pltpu.VMEM((F * R, 3 * C), BF16),
                pltpu.VMEM((F * R, slots), F32),
                pltpu.VMEM((F * R, slots), BF16),
                pltpu.VMEM((F * R, slots), BF16),
                pltpu.VMEM((2 * R, slots), BF16),
                pltpu.VMEM((F * R, C), F32),
                pltpu.SemaphoreType.DMA((8,)),
                pltpu.SemaphoreType.DMA((9,)),
                pltpu.SemaphoreType.DMA((9,)),
            ],
            compiler_params=pltpu.CompilerParams(collective_id=0, has_side_effects=True),
        )(
            tracers.reshape(F, R, C),
            courant_lon.reshape(L, R, C),
            courant_lat.reshape(L, R, C),
            cell_mass.reshape(L * R, C),
            donor_cell.reshape(nz, 1, K),
            donor_frac.reshape(2, nz, 1, K),
            target_cell.reshape(nz, 1, K),
            live_count.reshape(nz),
        )
        return merged.reshape(1, T, L, R, C) * scale.reshape(1, T, 1, R, C)

    lon = "lon"
    placed = (
        P("panel", None, None, "lat", lon),
        P("panel", None, "lat", lon),
        P("panel", None, "lat", lon),
        P("panel", None, "lat", lon),
        P("panel", "lat", lon, None, None),
        P(None, "panel", "lat", lon, None, None),
        P("panel", "lat", lon, None, None),
        P("panel", "lat", lon, None),
    )
    return jax.shard_map(
        body,
        mesh=mesh,
        in_specs=placed,
        out_specs=P("panel", None, None, "lat", lon),
        check_vma=False,
    )
```

```python
import jax
import jax.numpy as jnp
from jax import lax
from jax.experimental import pallas as pl
from jax.experimental.pallas import tpu as pltpu
from jax.sharding import PartitionSpec as P

F32 = jnp.float32
BF16 = jnp.bfloat16
MESH = pl.DeviceIdType.MESH

T = 4
L = 8
F = T * L
R = 8
C = 128
K = 64
FAR = 5
NX = 4
WEST, EAST, SOUTH, NORTH, NORTH_C, MASSES, MARGIN, SUM_FAR, SUM_NEAR, SUM_Z, DIRECT = range(11)


def left(x, by):
    by = by % C
    return x if by == 0 else pltpu.roll(x, (C - by) % C, x.ndim - 1)


def alphas(c):
    s = jnp.abs(c)
    m = 0.5 * s
    n = m - m * s * (2.0 / 3.0)
    n3 = 3.0 * n
    k1 = c * (1.0 - m - n3)
    k0 = c * (m - n3)
    ka = 2.0 * n3 * c
    u = k0 * (1.0 / 12.0)
    w = k1 * (1.0 / 12.0)
    pos = c > 0.0
    zero = jnp.zeros_like(c)
    near = 7.0 * (u + w) + ka
    far = 7.0 * u - w
    mid = 7.0 * w - u
    return (
        jnp.where(pos, -u, zero),
        jnp.where(pos, far, -w),
        jnp.where(pos, near, mid),
        jnp.where(pos, mid, near),
        jnp.where(pos, -w, far),
        jnp.where(pos, zero, -u),
    )


def betas(c, c_next):
    here, after = alphas(c), alphas(c_next)
    return [-here[0]] + [after[k - 1] - here[k] for k in range(1, 6)] + [after[5]]


def cubic(t):
    a, b, d = t + 1.0, t - 1.0, t - 2.0
    return (
        -t * b * d * (1.0 / 6.0),
        a * b * d * 0.5,
        -a * t * d * 0.5,
        a * t * b * (1.0 / 6.0),
    )


def pick(delta, weights):
    value = jnp.where(delta == 0, weights[0], 0.0)
    for i in range(1, 4):
        value = jnp.where(delta == i, weights[i], value)
    return value


def halves(x):
    high = x.astype(BF16)
    return high, (x - high.astype(F32)).astype(BF16)


def wait_all(ref, sem):
    pltpu.make_async_copy(ref, ref, sem).wait()


def kernel(nz, nlon, q_hbm, clon_hbm, clat_hbm, mass_hbm, donor_hbm, frac_hbm, target_hbm, live_hbm,
           out, scale_out, field, clon, clat, mass, donor, frac, target, live, send_w, send_e, recv_w, recv_e,
           cm_send, cm_recv, packet, arrived, rows, sum_far, sum_near, direct, sum_z, mass_old, base, latw, adv, onehot, colw,
           roww, lhs, mixed, scat_hi, scat_lo, rowmask, scattered, local_sem, send_sem, recv_sem):
    p = lax.axis_index("panel")
    z = lax.axis_index("lat")
    b = lax.axis_index("lon")
    x, y = lax.rem(b, NX), lax.div(b, NX)
    ny = nlon // NX
    other = 1 - p

    def at_z(step):
        return lax.rem(z + step, nz)

    west, east = lax.rem(b + nlon - 1, nlon), lax.rem(b + 1, nlon)
    south, north = at_z(nz - 1), at_z(1)

    loads = [
        pltpu.make_async_copy(q_hbm, field.at[:, pl.ds(R, R), :], local_sem.at[0]),
        pltpu.make_async_copy(clon_hbm, clon, local_sem.at[1]),
        pltpu.make_async_copy(clat_hbm, clat.at[:, pl.ds(0, R), :], local_sem.at[2]),
        pltpu.make_async_copy(mass_hbm, mass, local_sem.at[3]),
        pltpu.make_async_copy(donor_hbm, donor, local_sem.at[4]),
        pltpu.make_async_copy(frac_hbm, frac, local_sem.at[5]),
        pltpu.make_async_copy(target_hbm, target, local_sem.at[6]),
        pltpu.make_async_copy(live_hbm, live, local_sem.at[7]),
    ]
    barrier = pltpu.get_barrier_semaphore()
    far_first = sorted(range(nz), key=lambda i: -min(i, nz - i))
    partners = [(core, at_z(i), b) for i in far_first[:-1] for core in (other, p)] + [(other, z, b)]
    plane = [(i, j) for i in range(ny) for j in range(NX) if i + j > 0]
    plane.sort(key=lambda ij: -min(ij[0], ny - ij[0]) - min(ij[1], NX - ij[1]))

    def at_plane(i, j):
        return lax.rem(y + i, ny) * NX + lax.rem(x + j, NX)

    partners += [(p, z, at_plane(i, j)) for i, j in plane]
    for load in (loads[6], loads[7], loads[3], *loads[:3], *loads[4:6]):
        load.start()
    middle = range(4, nz - 3)
    is_first = (p == 1) & (z == 0) & (b == 0)
    in_middle = (z >= middle[0]) & (z <= middle[-1])
    sends_direct = [(at_plane(i, j) == 0) & in_middle for i, j in plane[:FAR]]
    direct_any = sends_direct[0]
    for one in sends_direct[1:]:
        direct_any = direct_any | one

    for partner in partners:
        pl.semaphore_signal(barrier, inc=1, device_id=partner, device_id_type=MESH)

    @pl.when(is_first)
    def _():
        for i, j in plane[:FAR]:
            place = (ny - i) % ny * NX + (NX - j) % NX

            @pl.loop(middle[0], middle[-1] + 1)
            def _(level):
                for core in range(2):
                    pl.semaphore_signal(barrier, inc=1, device_id=(core, level, place), device_id_type=MESH)

    lane = lax.broadcasted_iota(jnp.int32, (R, C), 1)
    lane16 = lax.broadcasted_iota(jnp.int32, (2 * R, C), 1)
    lane_row = lax.broadcasted_iota(jnp.int32, (1, C), 1)
    sub = lax.broadcasted_iota(jnp.int32, (2 * R, C), 0)
    column = lax.broadcasted_iota(jnp.int32, (C, C), 0)
    low, low16 = lane < K, lane16 < K

    loads[6].wait()
    loads[7].wait()

    def slots(read):
        return jnp.concatenate(
            [jnp.concatenate([read(v), read(v + 6)], axis=1) for v in range(6)], axis=0
        )

    spots = slots(lambda d: target[d])
    spot_col = spots & (C - 1)
    spot_row = spots >> 7
    live_rows = []
    for v in range(6):
        count = jnp.where(lane_row < K, live[v], live[v + 6])
        live_rows.append(jnp.where((lane_row & (K - 1)) < count, spot_row[v : v + 1, :], R))
    for v in range(6):
        cols = pl.ds(v * C, C)
        onehot[:, cols] = jnp.where(column == spot_col[v : v + 1, :], 1.0, 0.0).astype(BF16)
        rowmask[:, cols] = jnp.where(sub == live_rows[v], 1.0, 0.0).astype(BF16)
    filled = lax.dot_general(
        rowmask[...], onehot[...], (((1,), (1,)), ((), ())), preferred_element_type=F32
    )[0:R, :]

    loads[3].wait()
    by_row = jnp.concatenate([mass[pl.ds(r, L, stride=R), :] for r in range(R)], axis=0)
    mass_hi, mass_lo = halves(by_row)
    mass_at = jnp.dot(mass_hi, onehot[...], preferred_element_type=F32) + jnp.dot(
        mass_lo, onehot[...], preferred_element_type=F32
    )
    for v in range(6):
        total = jnp.zeros((L, C), F32)
        for r in range(R):
            total += jnp.where(
                live_rows[v] == r, mass_at[r * L : (r + 1) * L, v * C : (v + 1) * C], 0.0
            )
        turned = left(total, K)
        cm_send[v] = jnp.where(low, total, pltpu.roll(turned, 4, 0))[0:4, :]
        cm_send[v + 6] = jnp.where(low, turned, pltpu.roll(total, 4, 0))[0:4, :]

    loads[0].wait()
    loads[1].wait()
    loads[2].wait()
    own = [jnp.zeros((R, C), F32) for _ in range(4)]
    firsts = (0, 4, 124, 120)
    for f in range(F):
        tile = field[f, R : 2 * R, :]
        band = (lane >= 4 * f) & (lane < 4 * f + 4)
        own = [jnp.where(band, left(tile, first - 4 * f), o) for first, o in zip(firsts, own)]
    own_w, own_w2, own_e, own_e2 = own
    edge = [jnp.zeros((R, C), F32) for _ in range(4)]
    firsts = (0, 1, 124, 125)
    for l in range(L):
        tile = clon[l]
        band = (lane >= 4 * l) & (lane < 4 * l + 4)
        edge = [jnp.where(band, left(tile, first - 4 * l), o) for first, o in zip(firsts, edge)]
    edge = [o + pltpu.roll(o, 32, 1) for o in edge]
    c_w, c_w_next, c_e, c_e_next = [o + pltpu.roll(o, 64, 1) for o in edge]
    send_w[0] = own_w
    send_w[1] = c_w
    send_e[0] = own_e
    def prepare():
        loads[4].wait()
        loads[5].wait()
        cells = slots(lambda d: donor[d])
        start_col = cells & (C - 1)
        start_row = cells >> 7
        row_weights = cubic(slots(lambda d: frac[0, d]))
        col_weights = cubic(slots(lambda d: frac[1, d]))
        for r in range(R):
            roww[r, 0:6, :] = pick(r - start_row, row_weights)
        for v in range(6):
            cols = pl.ds(v * C, C)
            weights = pick(
                column - start_col[v : v + 1, :], [w[v : v + 1, :] for w in col_weights]
            )
            high, low_part = halves(weights)
            colw[0:C, cols] = high
            colw[C : 2 * C, cols] = high
            colw[2 * C : 3 * C, cols] = low_part

        inside = (lane >= 4) & (lane < 124)
        old = [jnp.zeros((R, C), F32) for _ in range(T)]
        for l in range(L):
            coef = [
                jnp.where(inside, o, 0.0) for o in betas(clon[l], left(clon[l], 1))
            ]
            for t in range(T):
                tile = field[t * L + l, R : 2 * R, :]
                old[t] += mass[l * R : (l + 1) * R, :] * tile
                value = tile
                for k in range(7):
                    value -= coef[k] * left(tile, k - 3)
                base[t * L + l] = value
        for t in range(T):
            mass_old[t] = old[t]

    late = z >= nz - 4
    pl.when(jnp.logical_not(late))(prepare)
    pl.semaphore_wait(barrier, len(partners) + jnp.where(direct_any, 1, 0))

    def remote(src, dst, which, device):
        return pltpu.make_async_remote_copy(
            src_ref=src,
            dst_ref=dst,
            send_sem=send_sem.at[which],
            recv_sem=recv_sem.at[which],
            device_id=device,
            device_id_type=MESH,
        )

    far_first = sorted(range(nz), key=lambda i: -min(i, nz - i))
    halo = [
        remote(send_w, recv_e, EAST, (p, z, west)),
        remote(send_e, recv_w, WEST, (p, z, east)),
        remote(field.at[:, pl.ds(13, 3), :], field.at[:, pl.ds(5, 3), :], SOUTH, (p, north, b)),
        remote(field.at[:, pl.ds(8, 3), :], field.at[:, pl.ds(16, 3), :], NORTH, (p, south, b)),
        remote(clat.at[:, pl.ds(0, 1), :], clat.at[:, pl.ds(R, 1), :], NORTH_C, (p, south, b)),
    ]
    for copy in halo[:2]:
        copy.start()
    for i in far_first[:5]:
        peer = at_z(i)
        remote(cm_send.at[peer], cm_recv.at[z], MASSES, (other, peer, b)).start()
    for copy in halo[2:]:
        copy.start()
    for i in far_first[5:]:
        peer = at_z(i)
        remote(cm_send.at[peer], cm_recv.at[z], MASSES, (other, peer, b)).start()

    pl.when(late)(prepare)
    for copy in halo[:2]:
        copy.wait()
    quarter = lane & 3
    halo_w = jnp.where(b == 0, 0.0, recv_w[0])
    halo_e = jnp.where(b == nlon - 1, 0.0, recv_e[0])
    halo_c = jnp.where(b == nlon - 1, 0.0, recv_e[1])
    c_e_next = jnp.where(quarter == 3, left(halo_c, -3), c_e_next)

    def packed(before, middle, after, coef):
        value = coef[3] * middle
        for k in range(7):
            s = k - 3
            if s < 0:
                cell = jnp.where(quarter < -s, left(before, 4 + s), left(middle, s))
            elif s > 0:
                cell = jnp.where(quarter >= 4 - s, left(after, s - 4), left(middle, s))
            else:
                continue
            value += coef[k] * cell
        return value

    change_w = packed(halo_w, own_w, own_w2, betas(c_w, c_w_next))
    change_e = packed(own_e2, own_e, halo_e, betas(c_e, c_e_next))

    for f in range(F):
        value = base[f] - jnp.where(lane < 4, left(change_w, 4 * f), 0.0)
        base[f] = value - jnp.where(lane >= 124, left(change_e, 4 * f + 4), 0.0)

    halo[4].wait()

    @pl.when(z == nz - 1)
    def _():
        clat[:, 8:9, :] = jnp.zeros((L, 1, C), F32)

    for l in range(L):
        for k, coef in enumerate(betas(clat[l, 0:8, :], clat[l, 1:9, :])):
            latw[l, k] = coef

    for copy in halo[2:4]:
        copy.wait()

    @pl.when(z == 0)
    def _():
        field[:, 5:8, :] = jnp.zeros((F, 3, C), F32)

    @pl.when(z == nz - 1)
    def _():
        field[:, 16:19, :] = jnp.zeros((F, 3, C), F32)

    keep = filled < 0.5
    mass_new = [jnp.zeros((R, C), F32) for _ in range(T)]
    for l in range(L):
        coef = [latw[l, k] for k in range(7)]
        kept = jnp.where(keep, mass[l * R : (l + 1) * R, :], 0.0)
        for t in range(T):
            f = t * L + l
            value = base[f]
            for k in range(7):
                value -= coef[k] * field[f, 5 + k : 13 + k, :]
            adv[f * R : (f + 1) * R, :] = value
            mass_new[t] += kept * value

    for r in range(R):
        high, low_part = halves(adv[pl.ds(r, F, stride=R), :])
        at = pl.ds(r * F, F)
        lhs[at, 0:C] = high
        lhs[at, C : 2 * C] = low_part
        lhs[at, 2 * C : 3 * C] = high
    mixed[...] = jnp.dot(lhs[...], colw[...], preferred_element_type=F32)
    for v in range(6):
        total = jnp.zeros((F, C), F32)
        for r in range(R):
            total += roww[r, v : v + 1, :] * mixed[r * F : (r + 1) * F, v * C : (v + 1) * C]
        first, second = total[0 : F // 2, :], total[F // 2 : F, :]
        packet[v] = jnp.where(low16, first, left(second, K))
        packet[v + 6] = jnp.where(low16, left(first, K), second)
    for i in far_first:
        peer = at_z(i)
        remote(packet.at[peer], arrived.at[z], MARGIN, (other, peer, b)).start()

    wait_all(cm_recv, recv_sem.at[MASSES])
    parts = [jnp.zeros((R, C), F32) for _ in range(2)]
    for d in range(12):
        four = cm_recv[d]
        eight = jnp.concatenate([four, left(four, K)], axis=0)
        eight = jnp.where(low, eight, left(eight, K))
        for half in range(2):
            parts[half] += eight * packet[d, half * R : (half + 1) * R, :]
    for half in range(2):
        mass_new[half] += jnp.where(low, parts[half], 0.0)
        mass_new[half + 2] += jnp.where(low, 0.0, parts[half])
    stacked = jnp.concatenate(
        [jnp.sum(m, axis=0, keepdims=True) for m in [mass_old[t] for t in range(T)] + mass_new], axis=0
    )
    sums = jnp.sum(stacked, axis=1, keepdims=True)
    row = jnp.sum(jnp.where(lane == sub[0:R, :], sums, 0.0), axis=0, keepdims=True)

    rows[0:1, :] = row
    rows[3:4, :] = jnp.zeros((1, C), F32)
    for n, (i, j) in enumerate(plane):
        device = (p, z, at_plane(i, j))
        if n < FAR:
            remote(rows.at[pl.ds(0, 1), :], sum_far.at[pl.ds(n, 1), :], SUM_FAR, device).start()

            @pl.when(sends_direct[n])
            def _():
                slot = (z - middle[0]) * 2 + p
                remote(rows.at[pl.ds(0, 1), :], direct.at[slot, pl.ds(n, 1), :], DIRECT, (1, 0, 0)).start()

        else:
            remote(rows.at[pl.ds(0, 1), :], sum_near.at[pl.ds(n - FAR, 1), :], SUM_NEAR, device).start()
    line = [(core, i) for i in far_first if i > 0 for core in (p, other)] + [(other, 0)]
    to_first = [(core == 1) & (b == 0) & (z == nz - i) if i in middle else None for core, i in line]
    wait_all(sum_near, recv_sem.at[SUM_NEAR])
    row = row + jnp.sum(sum_near[...], axis=0, keepdims=True)
    rows[2:3, :] = row

    def along_z(n, source):
        core, i = line[n]
        remote(rows.at[pl.ds(source, 1), :], sum_z.at[pl.ds(n, 1), :], SUM_Z, (core, at_z(i), b)).start()

    @pl.when((b == 0) & in_middle)
    def _():
        for n, special in enumerate(to_first):
            if special is not None:
                pl.when(special)(lambda n=n: along_z(n, 2))

    wait_all(sum_far, recv_sem.at[SUM_FAR])
    row = row + jnp.sum(sum_far[...], axis=0, keepdims=True)
    rows[1:2, :] = row
    for n, special in enumerate(to_first):
        if special is None:
            along_z(n, 1)
        else:
            pl.when(jnp.logical_not(special))(lambda n=n: along_z(n, 1))

    wait_all(arrived, recv_sem.at[MARGIN])
    for v in range(6):
        cols = pl.ds(v * C, C)
        one, two = arrived[v], arrived[v + 6]
        first = jnp.where(low16, one, left(two, K))
        second = jnp.where(low16, left(one, K), two)
        values = jnp.concatenate([first, second], axis=0)
        high = values.astype(BF16).astype(F32)
        low_part = values - high
        for r in range(R):
            at = pl.ds(r * F, F)
            here = live_rows[v] == r
            scat_hi[at, cols] = jnp.where(here, high, 0.0).astype(BF16)
            scat_lo[at, cols] = jnp.where(here, low_part, 0.0).astype(BF16)
    nt = (((1,), (1,)), ((), ()))
    scattered[...] = lax.dot_general(
        scat_hi[...], onehot[...], nt, preferred_element_type=F32
    ) + lax.dot_general(scat_lo[...], onehot[...], nt, preferred_element_type=F32)
    for f in range(F):
        at = pl.ds(f * R, R)
        out[f] = jnp.where(keep, adv[at, :], scattered[pl.ds(f, R, stride=F), :])

    @pl.when(is_first)
    def _():
        wait_all(direct, recv_sem.at[DIRECT])
        rows[3:4, :] = jnp.sum(jnp.sum(direct[...], axis=0), axis=0, keepdims=True)

    wait_all(sum_z, recv_sem.at[SUM_Z])
    row = row + (jnp.sum(sum_z[...], axis=0, keepdims=True) + rows[3:4, :])
    ratio = row / left(row, 4)
    for t in range(T):
        scale_out[t] = jnp.broadcast_to(ratio[:, t : t + 1], (R, C))

    wait_all(cm_send, send_sem.at[MASSES])
    wait_all(packet, send_sem.at[MARGIN])
    wait_all(sum_far, send_sem.at[SUM_FAR])
    wait_all(sum_near, send_sem.at[SUM_NEAR])

    @pl.when(direct_any)
    def _():
        wait_all(rows.at[pl.ds(0, 1), :], send_sem.at[DIRECT])

    wait_all(sum_z, send_sem.at[SUM_Z])


def solution(mesh):
    nz, nlon = mesh.shape["lat"], mesh.shape["lon"]
    ny = nlon // NX

    def body(tracers, courant_lon, courant_lat, cell_mass, donor_cell, donor_frac, target_cell, live_count):
        slots = nz * K
        hbm_spec = pl.BlockSpec(memory_space=pltpu.HBM)
        vmem_spec = pl.BlockSpec(memory_space=pltpu.VMEM)

        def run(*refs):
            kernel(nz, nlon, *refs)

        merged, scale = pl.pallas_call(
            run,
            out_shape=(
                pltpu.VMEM((F, R, C), F32),
                pltpu.VMEM((T, R, C), F32),
            ),
            in_specs=[hbm_spec] * 8,
            out_specs=(vmem_spec, vmem_spec),
            scratch_shapes=[
                pltpu.VMEM((F, 3 * R, C), F32),
                pltpu.VMEM((L, R, C), F32),
                pltpu.VMEM((L, 2 * R, C), F32),
                pltpu.VMEM((L * R, C), F32),
                pltpu.VMEM((nz, 1, K), jnp.int32),
                pltpu.VMEM((2, nz, 1, K), F32),
                pltpu.VMEM((nz, 1, K), jnp.int32),
                pltpu.SMEM((nz,), jnp.int32),
                pltpu.VMEM((2, R, C), F32),
                pltpu.VMEM((1, R, C), F32),
                pltpu.VMEM((1, R, C), F32),
                pltpu.VMEM((2, R, C), F32),
                pltpu.VMEM((nz, 4, C), F32),
                pltpu.VMEM((nz, 4, C), F32),
                pltpu.VMEM((nz, 2 * R, C), F32),
                pltpu.VMEM((nz, 2 * R, C), F32),
                pltpu.VMEM((4, C), F32),
                pltpu.VMEM((FAR, C), F32),
                pltpu.VMEM((nlon - 1 - FAR, C), F32),
                pltpu.VMEM((2 * (nz - 7), FAR, C), F32),
                pltpu.VMEM((2 * nz - 1, C), F32),
                pltpu.VMEM((T, R, C), F32),
                pltpu.VMEM((F, R, C), F32),
                pltpu.VMEM((L, 7, R, C), F32),
                pltpu.VMEM((F * R, C), F32),
                pltpu.VMEM((C, slots), BF16),
                pltpu.VMEM((3 * C, slots), BF16),
                pltpu.VMEM((R, R, C), F32),
                pltpu.VMEM((F * R, 3 * C), BF16),
                pltpu.VMEM((F * R, slots), F32),
                pltpu.VMEM((F * R, slots), BF16),
                pltpu.VMEM((F * R, slots), BF16),
                pltpu.VMEM((2 * R, slots), BF16),
                pltpu.VMEM((F * R, C), F32),
                pltpu.SemaphoreType.DMA((8,)),
                pltpu.SemaphoreType.DMA((11,)),
                pltpu.SemaphoreType.DMA((11,)),
            ],
            compiler_params=pltpu.CompilerParams(collective_id=0, has_side_effects=True),
        )(
            tracers.reshape(F, R, C),
            courant_lon.reshape(L, R, C),
            courant_lat.reshape(L, R, C),
            cell_mass.reshape(L * R, C),
            donor_cell.reshape(nz, 1, K),
            donor_frac.reshape(2, nz, 1, K),
            target_cell.reshape(nz, 1, K),
            live_count.reshape(nz),
        )
        return merged.reshape(1, T, L, R, C) * scale.reshape(1, T, 1, R, C)

    lon = "lon"
    placed = (
        P("panel", None, None, "lat", lon),
        P("panel", None, "lat", lon),
        P("panel", None, "lat", lon),
        P("panel", None, "lat", lon),
        P("panel", "lat", lon, None, None),
        P(None, "panel", "lat", lon, None, None),
        P("panel", "lat", lon, None, None),
        P("panel", "lat", lon, None),
    )
    return jax.shard_map(
        body,
        mesh=mesh,
        in_specs=placed,
        out_specs=P("panel", None, None, "lat", lon),
        check_vma=False,
    )
```

```python
import jax
import jax.numpy as jnp
from jax import lax
from jax.experimental import pallas as pl
from jax.experimental.pallas import tpu as pltpu
from jax.sharding import PartitionSpec as P

F32 = jnp.float32
BF16 = jnp.bfloat16
MESH = pl.DeviceIdType.MESH

T = 4
L = 8
F = T * L
R = 8
C = 128
K = 64
FAR = 12
NX = 4
WEST, EAST, SOUTH, NORTH, NORTH_C, MASSES, MARGIN, SUM_FAR, SUM_NEAR, SUM_Z, DIRECT = range(11)


def left(x, by):
    by = by % C
    return x if by == 0 else pltpu.roll(x, (C - by) % C, x.ndim - 1)


def alphas(c):
    s = jnp.abs(c)
    m = 0.5 * s
    n = m - m * s * (2.0 / 3.0)
    n3 = 3.0 * n
    k1 = c * (1.0 - m - n3)
    k0 = c * (m - n3)
    ka = 2.0 * n3 * c
    u = k0 * (1.0 / 12.0)
    w = k1 * (1.0 / 12.0)
    pos = c > 0.0
    zero = jnp.zeros_like(c)
    near = 7.0 * (u + w) + ka
    far = 7.0 * u - w
    mid = 7.0 * w - u
    return (
        jnp.where(pos, -u, zero),
        jnp.where(pos, far, -w),
        jnp.where(pos, near, mid),
        jnp.where(pos, mid, near),
        jnp.where(pos, -w, far),
        jnp.where(pos, zero, -u),
    )


def betas(c, c_next):
    here, after = alphas(c), alphas(c_next)
    return [-here[0]] + [after[k - 1] - here[k] for k in range(1, 6)] + [after[5]]


def cubic(t):
    a, b, d = t + 1.0, t - 1.0, t - 2.0
    return (
        -t * b * d * (1.0 / 6.0),
        a * b * d * 0.5,
        -a * t * d * 0.5,
        a * t * b * (1.0 / 6.0),
    )


def pick(delta, weights):
    value = jnp.where(delta == 0, weights[0], 0.0)
    for i in range(1, 4):
        value = jnp.where(delta == i, weights[i], value)
    return value


def halves(x):
    high = x.astype(BF16)
    return high, (x - high.astype(F32)).astype(BF16)


def wait_all(ref, sem):
    pltpu.make_async_copy(ref, ref, sem).wait()


def kernel(nz, nlon, q_hbm, clon_hbm, clat_hbm, mass_hbm, donor_hbm, frac_hbm, target_hbm, live_hbm,
           out, field, clon, clat, mass, donor, frac, target, live, send_w, send_e, recv_w, recv_e,
           cm_send, cm_recv, packet, arrived, rows, sum_far, sum_near, direct, sum_z, ends, filled, mass_old, base, latw, adv, onehot, colw,
           roww, lhs, mixed, scat_hi, scat_lo, rowmask, scattered, local_sem, send_sem, recv_sem):
    p = lax.axis_index("panel")
    z = lax.axis_index("lat")
    b = lax.axis_index("lon")
    x, y = lax.rem(b, NX), lax.div(b, NX)
    ny = nlon // NX
    other = 1 - p

    def at_z(step):
        return lax.rem(z + step, nz)

    west, east = lax.rem(b + nlon - 1, nlon), lax.rem(b + 1, nlon)
    south, north = at_z(nz - 1), at_z(1)

    loads = [
        pltpu.make_async_copy(q_hbm, field.at[:, pl.ds(R, R), :], local_sem.at[0]),
        pltpu.make_async_copy(clon_hbm, clon, local_sem.at[1]),
        pltpu.make_async_copy(clat_hbm, clat.at[:, pl.ds(0, R), :], local_sem.at[2]),
        pltpu.make_async_copy(mass_hbm, mass, local_sem.at[3]),
        pltpu.make_async_copy(donor_hbm, donor, local_sem.at[4]),
        pltpu.make_async_copy(frac_hbm, frac, local_sem.at[5]),
        pltpu.make_async_copy(target_hbm, target, local_sem.at[6]),
        pltpu.make_async_copy(live_hbm, live, local_sem.at[7]),
    ]
    barrier = pltpu.get_barrier_semaphore()
    far_first = sorted(range(nz), key=lambda i: -min(i, nz - i))
    partners = [(core, at_z(i), b) for i in far_first[:-1] for core in (other, p)] + [(other, z, b)]
    plane = [(i, j) for i in range(ny) for j in range(NX) if i + j > 0]
    plane.sort(key=lambda ij: -min(ij[0], ny - ij[0]) - min(ij[1], NX - ij[1]))

    def at_plane(i, j):
        return lax.rem(y + i, ny) * NX + lax.rem(x + j, NX)

    partners += [(p, z, at_plane(i, j)) for i, j in plane]
    for load in (loads[6], loads[7], loads[3], *loads[:3], *loads[4:6]):
        load.start()
    middle = range(4, nz - 3)
    is_first = (p == 1) & (z == 0) & (b == 0)
    in_middle = (z >= middle[0]) & (z <= middle[-1])
    sends_direct = [(at_plane(i, j) == 0) & in_middle for i, j in plane[:FAR]]
    direct_any = sends_direct[0]
    for one in sends_direct[1:]:
        direct_any = direct_any | one

    for partner in partners:
        pl.semaphore_signal(barrier, inc=1, device_id=partner, device_id_type=MESH)

    @pl.when(is_first)
    def _():
        for i, j in plane[:FAR]:
            place = (ny - i) % ny * NX + (NX - j) % NX

            @pl.loop(middle[0], middle[-1] + 1)
            def _(level):
                for core in range(2):
                    pl.semaphore_signal(barrier, inc=1, device_id=(core, level, place), device_id_type=MESH)

    lane = lax.broadcasted_iota(jnp.int32, (R, C), 1)
    lane16 = lax.broadcasted_iota(jnp.int32, (2 * R, C), 1)
    lane_row = lax.broadcasted_iota(jnp.int32, (1, C), 1)
    sub = lax.broadcasted_iota(jnp.int32, (2 * R, C), 0)
    column = lax.broadcasted_iota(jnp.int32, (C, C), 0)
    low, low16 = lane < K, lane16 < K

    loads[6].wait()
    loads[7].wait()

    def slots(read):
        return jnp.concatenate(
            [jnp.concatenate([read(v), read(v + 6)], axis=1) for v in range(6)], axis=0
        )

    spots = slots(lambda d: target[d])
    spot_col = spots & (C - 1)
    spot_row = spots >> 7
    live_rows = []
    for v in range(6):
        count = jnp.where(lane_row < K, live[v], live[v + 6])
        live_rows.append(jnp.where((lane_row & (K - 1)) < count, spot_row[v : v + 1, :], R))
    for v in range(6):
        cols = pl.ds(v * C, C)
        onehot[:, cols] = jnp.where(column == spot_col[v : v + 1, :], 1.0, 0.0).astype(BF16)

    loads[3].wait()
    by_row = jnp.concatenate([mass[pl.ds(r, L, stride=R), :] for r in range(R)], axis=0)
    mass_hi, mass_lo = halves(by_row)
    mass_at = jnp.dot(mass_hi, onehot[...], preferred_element_type=F32) + jnp.dot(
        mass_lo, onehot[...], preferred_element_type=F32
    )
    for v in range(6):
        total = jnp.zeros((L, C), F32)
        for r in range(R):
            total += jnp.where(
                live_rows[v] == r, mass_at[r * L : (r + 1) * L, v * C : (v + 1) * C], 0.0
            )
        turned = left(total, K)
        cm_send[v] = jnp.where(low, total, pltpu.roll(turned, 4, 0))[0:4, :]
        cm_send[v + 6] = jnp.where(low, turned, pltpu.roll(total, 4, 0))[0:4, :]

    loads[0].wait()
    loads[1].wait()
    loads[2].wait()

    def pack_ends():
        own = [jnp.zeros((R, C), F32) for _ in range(4)]
        firsts = (0, 4, 124, 120)
        for f in range(F):
            tile = field[f, R : 2 * R, :]
            band = (lane >= 4 * f) & (lane < 4 * f + 4)
            own = [jnp.where(band, left(tile, first - 4 * f), o) for first, o in zip(firsts, own)]
        edge = [jnp.zeros((R, C), F32) for _ in range(4)]
        firsts = (0, 1, 124, 125)
        for l in range(L):
            tile = clon[l]
            band = (lane >= 4 * l) & (lane < 4 * l + 4)
            edge = [jnp.where(band, left(tile, first - 4 * l), o) for first, o in zip(firsts, edge)]
        edge = [o + pltpu.roll(o, 32, 1) for o in edge]
        edge = [o + pltpu.roll(o, 64, 1) for o in edge]
        for n, tile in enumerate(own + edge):
            ends[n] = tile
        send_w[0] = own[0]
        send_w[1] = edge[0]
        send_e[0] = own[2]

    def prepare():
        loads[4].wait()
        loads[5].wait()
        cells = slots(lambda d: donor[d])
        start_col = cells & (C - 1)
        start_row = cells >> 7
        row_weights = cubic(slots(lambda d: frac[0, d]))
        col_weights = cubic(slots(lambda d: frac[1, d]))
        for r in range(R):
            roww[r, 0:6, :] = pick(r - start_row, row_weights)
        for v in range(6):
            cols = pl.ds(v * C, C)
            weights = pick(
                column - start_col[v : v + 1, :], [w[v : v + 1, :] for w in col_weights]
            )
            high, low_part = halves(weights)
            colw[0:C, cols] = high
            colw[C : 2 * C, cols] = high
            colw[2 * C : 3 * C, cols] = low_part

        for v in range(6):
            rowmask[:, pl.ds(v * C, C)] = jnp.where(sub == live_rows[v], 1.0, 0.0).astype(BF16)
        filled[...] = lax.dot_general(
            rowmask[...], onehot[...], (((1,), (1,)), ((), ())), preferred_element_type=F32
        )[0:R, :]

        inside = (lane >= 4) & (lane < 124)
        old = [jnp.zeros((R, C), F32) for _ in range(T)]
        for l in range(L):
            coef = [
                jnp.where(inside, o, 0.0) for o in betas(clon[l], left(clon[l], 1))
            ]
            for t in range(T):
                tile = field[t * L + l, R : 2 * R, :]
                old[t] += mass[l * R : (l + 1) * R, :] * tile
                value = tile
                for k in range(7):
                    value -= coef[k] * left(tile, k - 3)
                base[t * L + l] = value
        for t in range(T):
            mass_old[t] = old[t]

    pack_ends()

    late = (z >= nz - 2) & (y >= ny // 2) & (y < ny - 1)
    pl.when(jnp.logical_not(late))(prepare)
    pl.semaphore_wait(barrier, len(partners) + jnp.where(direct_any, 1, 0))

    def remote(src, dst, which, device):
        return pltpu.make_async_remote_copy(
            src_ref=src,
            dst_ref=dst,
            send_sem=send_sem.at[which],
            recv_sem=recv_sem.at[which],
            device_id=device,
            device_id_type=MESH,
        )

    far_first = sorted(range(nz), key=lambda i: -min(i, nz - i))
    halo = [
        remote(send_w, recv_e, EAST, (p, z, west)),
        remote(send_e, recv_w, WEST, (p, z, east)),
        remote(field.at[:, pl.ds(13, 3), :], field.at[:, pl.ds(5, 3), :], SOUTH, (p, north, b)),
        remote(field.at[:, pl.ds(8, 3), :], field.at[:, pl.ds(16, 3), :], NORTH, (p, south, b)),
        remote(clat.at[:, pl.ds(0, 1), :], clat.at[:, pl.ds(R, 1), :], NORTH_C, (p, south, b)),
    ]
    def send_masses(steps):
        for i in steps:
            peer = at_z(i)
            remote(cm_send.at[peer], cm_recv.at[z], MASSES, (other, peer, b)).start()

    def start(copies):
        for copy in copies:
            copy.start()

    start(halo[:2])
    send_masses(far_first[:5])
    start(halo[2:])
    send_masses(far_first[5:])
    pl.when(late)(prepare)

    for copy in halo[:2]:
        copy.wait()
    own_w, own_w2, own_e, own_e2, c_w, c_w_next, c_e, c_e_next = (ends[n] for n in range(8))
    quarter = lane & 3
    halo_w = jnp.where(b == 0, 0.0, recv_w[0])
    halo_e = jnp.where(b == nlon - 1, 0.0, recv_e[0])
    halo_c = jnp.where(b == nlon - 1, 0.0, recv_e[1])
    c_e_next = jnp.where(quarter == 3, left(halo_c, -3), c_e_next)

    def packed(before, middle, after, coef):
        value = coef[3] * middle
        for k in range(7):
            s = k - 3
            if s < 0:
                cell = jnp.where(quarter < -s, left(before, 4 + s), left(middle, s))
            elif s > 0:
                cell = jnp.where(quarter >= 4 - s, left(after, s - 4), left(middle, s))
            else:
                continue
            value += coef[k] * cell
        return value

    change_w = packed(halo_w, own_w, own_w2, betas(c_w, c_w_next))
    change_e = packed(own_e2, own_e, halo_e, betas(c_e, c_e_next))

    for f in range(F):
        value = base[f] - jnp.where(lane < 4, left(change_w, 4 * f), 0.0)
        base[f] = value - jnp.where(lane >= 124, left(change_e, 4 * f + 4), 0.0)

    halo[4].wait()

    @pl.when(z == nz - 1)
    def _():
        clat[:, 8:9, :] = jnp.zeros((L, 1, C), F32)

    for l in range(L):
        for k, coef in enumerate(betas(clat[l, 0:8, :], clat[l, 1:9, :])):
            latw[l, k] = coef

    for copy in halo[2:4]:
        copy.wait()

    @pl.when(z == 0)
    def _():
        field[:, 5:8, :] = jnp.zeros((F, 3, C), F32)

    @pl.when(z == nz - 1)
    def _():
        field[:, 16:19, :] = jnp.zeros((F, 3, C), F32)

    keep = filled[...] < 0.5
    mass_new = [jnp.zeros((R, C), F32) for _ in range(T)]
    for l in range(L):
        coef = [latw[l, k] for k in range(7)]
        kept = jnp.where(keep, mass[l * R : (l + 1) * R, :], 0.0)
        for t in range(T):
            f = t * L + l
            value = base[f]
            for k in range(7):
                value -= coef[k] * field[f, 5 + k : 13 + k, :]
            adv[f * R : (f + 1) * R, :] = value
            mass_new[t] += kept * value

    for r in range(R):
        high, low_part = halves(adv[pl.ds(r, F, stride=R), :])
        at = pl.ds(r * F, F)
        lhs[at, 0:C] = high
        lhs[at, C : 2 * C] = low_part
        lhs[at, 2 * C : 3 * C] = high
    mixed[...] = jnp.dot(lhs[...], colw[...], preferred_element_type=F32)
    for v in range(6):
        total = jnp.zeros((F, C), F32)
        for r in range(R):
            total += roww[r, v : v + 1, :] * mixed[r * F : (r + 1) * F, v * C : (v + 1) * C]
        first, second = total[0 : F // 2, :], total[F // 2 : F, :]
        packet[v] = jnp.where(low16, first, left(second, K))
        packet[v + 6] = jnp.where(low16, left(first, K), second)
    for i in far_first:
        peer = at_z(i)
        remote(packet.at[peer], arrived.at[z], MARGIN, (other, peer, b)).start()

    wait_all(cm_recv, recv_sem.at[MASSES])
    parts = [jnp.zeros((R, C), F32) for _ in range(2)]
    for d in range(12):
        four = cm_recv[d]
        eight = jnp.concatenate([four, left(four, K)], axis=0)
        eight = jnp.where(low, eight, left(eight, K))
        for half in range(2):
            parts[half] += eight * packet[d, half * R : (half + 1) * R, :]
    for half in range(2):
        mass_new[half] += jnp.where(low, parts[half], 0.0)
        mass_new[half + 2] += jnp.where(low, 0.0, parts[half])
    stacked = jnp.concatenate(
        [jnp.sum(m, axis=0, keepdims=True) for m in [mass_old[t] for t in range(T)] + mass_new], axis=0
    )
    sums = jnp.sum(stacked, axis=1, keepdims=True)
    row = jnp.sum(jnp.where(lane == sub[0:R, :], sums, 0.0), axis=0, keepdims=True)

    rows[0:1, :] = row
    rows[3:4, :] = jnp.zeros((1, C), F32)
    for n, (i, j) in enumerate(plane):
        device = (p, z, at_plane(i, j))
        if n < FAR:
            remote(rows.at[pl.ds(0, 1), :], sum_far.at[pl.ds(n, 1), :], SUM_FAR, device).start()

            @pl.when(sends_direct[n])
            def _():
                slot = (z - middle[0]) * 2 + p
                remote(rows.at[pl.ds(0, 1), :], direct.at[slot, pl.ds(n, 1), :], DIRECT, (1, 0, 0)).start()

        else:
            remote(rows.at[pl.ds(0, 1), :], sum_near.at[pl.ds(n - FAR, 1), :], SUM_NEAR, device).start()
    line = [(core, i) for i in far_first if i > 0 for core in (p, other)] + [(other, 0)]
    to_first = [(core == 1) & (b == 0) & (z == nz - i) if i in middle else None for core, i in line]
    wait_all(sum_near, recv_sem.at[SUM_NEAR])
    row = row + jnp.sum(sum_near[...], axis=0, keepdims=True)
    rows[2:3, :] = row

    def along_z(n, source):
        core, i = line[n]
        remote(rows.at[pl.ds(source, 1), :], sum_z.at[pl.ds(n, 1), :], SUM_Z, (core, at_z(i), b)).start()

    @pl.when((b == 0) & in_middle)
    def _():
        for n, special in enumerate(to_first):
            if special is not None:
                pl.when(special)(lambda n=n: along_z(n, 2))

    wait_all(sum_far, recv_sem.at[SUM_FAR])
    row = row + jnp.sum(sum_far[...], axis=0, keepdims=True)
    rows[1:2, :] = row
    for n, special in enumerate(to_first):
        if special is None:
            along_z(n, 1)
        else:
            pl.when(jnp.logical_not(special))(lambda n=n: along_z(n, 1))

    wait_all(arrived, recv_sem.at[MARGIN])
    for v in range(6):
        cols = pl.ds(v * C, C)
        one, two = arrived[v], arrived[v + 6]
        first = jnp.where(low16, one, left(two, K))
        second = jnp.where(low16, left(one, K), two)
        values = jnp.concatenate([first, second], axis=0)
        high = values.astype(BF16).astype(F32)
        low_part = values - high
        for r in range(R):
            at = pl.ds(r * F, F)
            here = live_rows[v] == r
            scat_hi[at, cols] = jnp.where(here, high, 0.0).astype(BF16)
            scat_lo[at, cols] = jnp.where(here, low_part, 0.0).astype(BF16)
    nt = (((1,), (1,)), ((), ()))
    scattered[...] = lax.dot_general(
        scat_hi[...], onehot[...], nt, preferred_element_type=F32
    ) + lax.dot_general(scat_lo[...], onehot[...], nt, preferred_element_type=F32)
    for f in range(F):
        at = pl.ds(f * R, R)
        adv[at, :] = jnp.where(keep, adv[at, :], scattered[pl.ds(f, R, stride=F), :])

    @pl.when(is_first)
    def _():
        wait_all(direct, recv_sem.at[DIRECT])
        rows[3:4, :] = jnp.sum(jnp.sum(direct[...], axis=0), axis=0, keepdims=True)

    wait_all(sum_z, recv_sem.at[SUM_Z])
    row = row + (jnp.sum(sum_z[...], axis=0, keepdims=True) + rows[3:4, :])
    ratio = row / left(row, 4)
    for t in range(T):
        scale = jnp.broadcast_to(ratio[:, t : t + 1], (R, C))
        for l in range(L):
            f = t * L + l
            out[f] = adv[f * R : (f + 1) * R, :] * scale

    wait_all(cm_send, send_sem.at[MASSES])
    wait_all(packet, send_sem.at[MARGIN])
    wait_all(sum_far, send_sem.at[SUM_FAR])
    wait_all(sum_near, send_sem.at[SUM_NEAR])

    @pl.when(direct_any)
    def _():
        wait_all(rows.at[pl.ds(0, 1), :], send_sem.at[DIRECT])

    wait_all(sum_z, send_sem.at[SUM_Z])


def solution(mesh):
    nz, nlon = mesh.shape["lat"], mesh.shape["lon"]
    ny = nlon // NX

    def body(tracers, courant_lon, courant_lat, cell_mass, donor_cell, donor_frac, target_cell, live_count):
        slots = nz * K
        hbm_spec = pl.BlockSpec(memory_space=pltpu.HBM)
        vmem_spec = pl.BlockSpec(memory_space=pltpu.VMEM)

        def run(*refs):
            kernel(nz, nlon, *refs)

        result = pl.pallas_call(
            run,
            out_shape=pltpu.VMEM((F, R, C), F32),
            in_specs=[hbm_spec] * 8,
            out_specs=vmem_spec,
            scratch_shapes=[
                pltpu.VMEM((F, 3 * R, C), F32),
                pltpu.VMEM((L, R, C), F32),
                pltpu.VMEM((L, 2 * R, C), F32),
                pltpu.VMEM((L * R, C), F32),
                pltpu.VMEM((nz, 1, K), jnp.int32),
                pltpu.VMEM((2, nz, 1, K), F32),
                pltpu.VMEM((nz, 1, K), jnp.int32),
                pltpu.SMEM((nz,), jnp.int32),
                pltpu.VMEM((2, R, C), F32),
                pltpu.VMEM((1, R, C), F32),
                pltpu.VMEM((1, R, C), F32),
                pltpu.VMEM((2, R, C), F32),
                pltpu.VMEM((nz, 4, C), F32),
                pltpu.VMEM((nz, 4, C), F32),
                pltpu.VMEM((nz, 2 * R, C), F32),
                pltpu.VMEM((nz, 2 * R, C), F32),
                pltpu.VMEM((4, C), F32),
                pltpu.VMEM((FAR, C), F32),
                pltpu.VMEM((nlon - 1 - FAR, C), F32),
                pltpu.VMEM((2 * (nz - 7), FAR, C), F32),
                pltpu.VMEM((2 * nz - 1, C), F32),
                pltpu.VMEM((8, R, C), F32),
                pltpu.VMEM((R, C), F32),
                pltpu.VMEM((T, R, C), F32),
                pltpu.VMEM((F, R, C), F32),
                pltpu.VMEM((L, 7, R, C), F32),
                pltpu.VMEM((F * R, C), F32),
                pltpu.VMEM((C, slots), BF16),
                pltpu.VMEM((3 * C, slots), BF16),
                pltpu.VMEM((R, R, C), F32),
                pltpu.VMEM((F * R, 3 * C), BF16),
                pltpu.VMEM((F * R, slots), F32),
                pltpu.VMEM((F * R, slots), BF16),
                pltpu.VMEM((F * R, slots), BF16),
                pltpu.VMEM((2 * R, slots), BF16),
                pltpu.VMEM((F * R, C), F32),
                pltpu.SemaphoreType.DMA((8,)),
                pltpu.SemaphoreType.DMA((11,)),
                pltpu.SemaphoreType.DMA((11,)),
            ],
            compiler_params=pltpu.CompilerParams(collective_id=0, has_side_effects=True),
        )(
            tracers.reshape(F, R, C),
            courant_lon.reshape(L, R, C),
            courant_lat.reshape(L, R, C),
            cell_mass.reshape(L * R, C),
            donor_cell.reshape(nz, 1, K),
            donor_frac.reshape(2, nz, 1, K),
            target_cell.reshape(nz, 1, K),
            live_count.reshape(nz),
        )
        return result.reshape(1, T, L, R, C)

    lon = "lon"
    placed = (
        P("panel", None, None, "lat", lon),
        P("panel", None, "lat", lon),
        P("panel", None, "lat", lon),
        P("panel", None, "lat", lon),
        P("panel", "lat", lon, None, None),
        P(None, "panel", "lat", lon, None, None),
        P("panel", "lat", lon, None, None),
        P("panel", "lat", lon, None),
    )
    return jax.shard_map(
        body,
        mesh=mesh,
        in_specs=placed,
        out_specs=P("panel", None, None, "lat", lon),
        check_vma=False,
    )
```

```python
import jax
import jax.numpy as jnp
from jax import lax
from jax.experimental import pallas as pl
from jax.experimental.pallas import tpu as pltpu
from jax.sharding import PartitionSpec as P

F32 = jnp.float32
BF16 = jnp.bfloat16
MESH = pl.DeviceIdType.MESH

T = 4
L = 8
F = T * L
R = 8
C = 128
K = 64
FAR = 12
NX = 4
WEST, EAST, SOUTH, NORTH, NORTH_C, MASSES, MARGIN, SUM_FAR, SUM_NEAR, SUM_Z, DIRECT = range(11)


def left(x, by):
    by = by % C
    return x if by == 0 else pltpu.roll(x, (C - by) % C, x.ndim - 1)


def alphas(c):
    s = jnp.abs(c)
    m = 0.5 * s
    n = m - m * s * (2.0 / 3.0)
    n3 = 3.0 * n
    k1 = c * (1.0 - m - n3)
    k0 = c * (m - n3)
    ka = 2.0 * n3 * c
    u = k0 * (1.0 / 12.0)
    w = k1 * (1.0 / 12.0)
    pos = c > 0.0
    zero = jnp.zeros_like(c)
    near = 7.0 * (u + w) + ka
    far = 7.0 * u - w
    mid = 7.0 * w - u
    return (
        jnp.where(pos, -u, zero),
        jnp.where(pos, far, -w),
        jnp.where(pos, near, mid),
        jnp.where(pos, mid, near),
        jnp.where(pos, -w, far),
        jnp.where(pos, zero, -u),
    )


def betas(c, c_next):
    here, after = alphas(c), alphas(c_next)
    return [-here[0]] + [after[k - 1] - here[k] for k in range(1, 6)] + [after[5]]


def cubic(t):
    a, b, d = t + 1.0, t - 1.0, t - 2.0
    return (
        -t * b * d * (1.0 / 6.0),
        a * b * d * 0.5,
        -a * t * d * 0.5,
        a * t * b * (1.0 / 6.0),
    )


def pick(delta, weights):
    value = jnp.where(delta == 0, weights[0], 0.0)
    for i in range(1, 4):
        value = jnp.where(delta == i, weights[i], value)
    return value


def halves(x):
    high = x.astype(BF16)
    return high, (x - high.astype(F32)).astype(BF16)


def wait_all(ref, sem):
    pltpu.make_async_copy(ref, ref, sem).wait()


def kernel(nz, nlon, q_hbm, clon_hbm, clat_hbm, mass_hbm, donor_hbm, frac_hbm, target_hbm, live_hbm,
           out, field, clon, clat, mass, donor, frac, target, live, send_w, send_e, recv_w, recv_e,
           cm_send, cm_recv, packet, arrived, rows, sum_far, sum_near, direct, sum_z, ends, filled, mass_old, base, latw, adv, onehot, colw,
           roww, lhs, mixed, scat_hi, scat_lo, rowmask, scattered, local_sem, send_sem, recv_sem):
    p = lax.axis_index("panel")
    z = lax.axis_index("lat")
    b = lax.axis_index("lon")
    x, y = lax.rem(b, NX), lax.div(b, NX)
    ny = nlon // NX
    other = 1 - p

    def at_z(step):
        return lax.rem(z + step, nz)

    west, east = lax.rem(b + nlon - 1, nlon), lax.rem(b + 1, nlon)
    south, north = at_z(nz - 1), at_z(1)

    loads = [
        pltpu.make_async_copy(q_hbm, field.at[:, pl.ds(R, R), :], local_sem.at[0]),
        pltpu.make_async_copy(clon_hbm, clon, local_sem.at[1]),
        pltpu.make_async_copy(clat_hbm, clat.at[:, pl.ds(0, R), :], local_sem.at[2]),
        pltpu.make_async_copy(mass_hbm, mass, local_sem.at[3]),
        pltpu.make_async_copy(donor_hbm, donor, local_sem.at[4]),
        pltpu.make_async_copy(frac_hbm, frac, local_sem.at[5]),
        pltpu.make_async_copy(target_hbm, target, local_sem.at[6]),
        pltpu.make_async_copy(live_hbm, live, local_sem.at[7]),
    ]
    barrier = pltpu.get_barrier_semaphore()
    far_first = sorted(range(nz), key=lambda i: -min(i, nz - i))
    partners = [(core, at_z(i), b) for i in far_first[:-1] for core in (other, p)] + [(other, z, b)]
    plane = [(i, j) for i in range(ny) for j in range(NX) if i + j > 0]
    plane.sort(key=lambda ij: -min(ij[0], ny - ij[0]) - min(ij[1], NX - ij[1]))

    def at_plane(i, j):
        return lax.rem(y + i, ny) * NX + lax.rem(x + j, NX)

    partners += [(p, z, at_plane(i, j)) for i, j in plane]
    for load in (loads[6], loads[7], loads[3], *loads[:3], *loads[4:6]):
        load.start()
    middle = range(3, nz - 2)
    is_first = (p == 1) & (z == 0) & (b == 0)
    in_middle = (z >= middle[0]) & (z <= middle[-1])
    sends_direct = [(at_plane(i, j) == 0) & in_middle for i, j in plane[:FAR]]
    direct_any = sends_direct[0]
    for one in sends_direct[1:]:
        direct_any = direct_any | one

    for partner in partners:
        pl.semaphore_signal(barrier, inc=1, device_id=partner, device_id_type=MESH)

    @pl.when(is_first)
    def _():
        for i, j in plane[:FAR]:
            place = (ny - i) % ny * NX + (NX - j) % NX

            @pl.loop(middle[0], middle[-1] + 1)
            def _(level):
                for core in range(2):
                    pl.semaphore_signal(barrier, inc=1, device_id=(core, level, place), device_id_type=MESH)

    lane = lax.broadcasted_iota(jnp.int32, (R, C), 1)
    lane16 = lax.broadcasted_iota(jnp.int32, (2 * R, C), 1)
    lane_row = lax.broadcasted_iota(jnp.int32, (1, C), 1)
    sub = lax.broadcasted_iota(jnp.int32, (2 * R, C), 0)
    column = lax.broadcasted_iota(jnp.int32, (C, C), 0)
    low, low16 = lane < K, lane16 < K

    loads[6].wait()
    loads[7].wait()

    def slots(read):
        return jnp.concatenate(
            [jnp.concatenate([read(v), read(v + 6)], axis=1) for v in range(6)], axis=0
        )

    spots = slots(lambda d: target[d])
    spot_col = spots & (C - 1)
    spot_row = spots >> 7
    live_rows = []
    for v in range(6):
        count = jnp.where(lane_row < K, live[v], live[v + 6])
        live_rows.append(jnp.where((lane_row & (K - 1)) < count, spot_row[v : v + 1, :], R))
    for v in range(6):
        cols = pl.ds(v * C, C)
        onehot[:, cols] = jnp.where(column == spot_col[v : v + 1, :], 1.0, 0.0).astype(BF16)

    loads[3].wait()
    by_row = jnp.concatenate([mass[pl.ds(r, L, stride=R), :] for r in range(R)], axis=0)
    mass_hi, mass_lo = halves(by_row)
    mass_at = jnp.dot(mass_hi, onehot[...], preferred_element_type=F32) + jnp.dot(
        mass_lo, onehot[...], preferred_element_type=F32
    )
    for v in range(6):
        total = jnp.zeros((L, C), F32)
        for r in range(R):
            total += jnp.where(
                live_rows[v] == r, mass_at[r * L : (r + 1) * L, v * C : (v + 1) * C], 0.0
            )
        turned = left(total, K)
        cm_send[v] = jnp.where(low, total, pltpu.roll(turned, 4, 0))[0:4, :]
        cm_send[v + 6] = jnp.where(low, turned, pltpu.roll(total, 4, 0))[0:4, :]

    loads[0].wait()
    loads[1].wait()
    loads[2].wait()

    def pack_ends():
        own = [jnp.zeros((R, C), F32) for _ in range(4)]
        firsts = (0, 4, 124, 120)
        for f in range(F):
            tile = field[f, R : 2 * R, :]
            band = (lane >= 4 * f) & (lane < 4 * f + 4)
            own = [jnp.where(band, left(tile, first - 4 * f), o) for first, o in zip(firsts, own)]
        edge = [jnp.zeros((R, C), F32) for _ in range(4)]
        firsts = (0, 1, 124, 125)
        for l in range(L):
            tile = clon[l]
            band = (lane >= 4 * l) & (lane < 4 * l + 4)
            edge = [jnp.where(band, left(tile, first - 4 * l), o) for first, o in zip(firsts, edge)]
        edge = [o + pltpu.roll(o, 32, 1) for o in edge]
        edge = [o + pltpu.roll(o, 64, 1) for o in edge]
        for n, tile in enumerate(own + edge):
            ends[n] = tile
        send_w[0] = own[0]
        send_w[1] = edge[0]
        send_e[0] = own[2]

    def prepare():
        loads[4].wait()
        loads[5].wait()
        cells = slots(lambda d: donor[d])
        start_col = cells & (C - 1)
        start_row = cells >> 7
        row_weights = cubic(slots(lambda d: frac[0, d]))
        col_weights = cubic(slots(lambda d: frac[1, d]))
        for r in range(R):
            roww[r, 0:6, :] = pick(r - start_row, row_weights)
        for v in range(6):
            cols = pl.ds(v * C, C)
            weights = pick(
                column - start_col[v : v + 1, :], [w[v : v + 1, :] for w in col_weights]
            )
            high, low_part = halves(weights)
            colw[0:C, cols] = high
            colw[C : 2 * C, cols] = high
            colw[2 * C : 3 * C, cols] = low_part

        for v in range(6):
            rowmask[:, pl.ds(v * C, C)] = jnp.where(sub == live_rows[v], 1.0, 0.0).astype(BF16)
        filled[...] = lax.dot_general(
            rowmask[...], onehot[...], (((1,), (1,)), ((), ())), preferred_element_type=F32
        )[0:R, :]

        inside = (lane >= 4) & (lane < 124)
        old = [jnp.zeros((R, C), F32) for _ in range(T)]
        for l in range(L):
            coef = [
                jnp.where(inside, o, 0.0) for o in betas(clon[l], left(clon[l], 1))
            ]
            for t in range(T):
                tile = field[t * L + l, R : 2 * R, :]
                old[t] += mass[l * R : (l + 1) * R, :] * tile
                value = tile
                for k in range(7):
                    value -= coef[k] * left(tile, k - 3)
                base[t * L + l] = value
        for t in range(T):
            mass_old[t] = old[t]

    pack_ends()

    late = (z >= nz - 2) & (y >= ny // 2) & (y < ny - 1)
    pl.when(jnp.logical_not(late))(prepare)
    pl.semaphore_wait(barrier, len(partners) + jnp.where(direct_any, 1, 0))

    def remote(src, dst, which, device):
        return pltpu.make_async_remote_copy(
            src_ref=src,
            dst_ref=dst,
            send_sem=send_sem.at[which],
            recv_sem=recv_sem.at[which],
            device_id=device,
            device_id_type=MESH,
        )

    far_first = sorted(range(nz), key=lambda i: -min(i, nz - i))
    halo = [
        remote(send_w, recv_e, EAST, (p, z, west)),
        remote(send_e, recv_w, WEST, (p, z, east)),
        remote(field.at[:, pl.ds(13, 3), :], field.at[:, pl.ds(5, 3), :], SOUTH, (p, north, b)),
        remote(field.at[:, pl.ds(8, 3), :], field.at[:, pl.ds(16, 3), :], NORTH, (p, south, b)),
        remote(clat.at[:, pl.ds(0, 1), :], clat.at[:, pl.ds(R, 1), :], NORTH_C, (p, south, b)),
    ]
    def send_masses(steps):
        for i in steps:
            peer = at_z(i)
            remote(cm_send.at[peer], cm_recv.at[z], MASSES, (other, peer, b)).start()

    def start(copies):
        for copy in copies:
            copy.start()

    start(halo[:2])
    send_masses(far_first[:5])
    start(halo[2:])
    send_masses(far_first[5:])
    pl.when(late)(prepare)

    for copy in halo[:2]:
        copy.wait()
    own_w, own_w2, own_e, own_e2, c_w, c_w_next, c_e, c_e_next = (ends[n] for n in range(8))
    quarter = lane & 3
    halo_w = jnp.where(b == 0, 0.0, recv_w[0])
    halo_e = jnp.where(b == nlon - 1, 0.0, recv_e[0])
    halo_c = jnp.where(b == nlon - 1, 0.0, recv_e[1])
    c_e_next = jnp.where(quarter == 3, left(halo_c, -3), c_e_next)

    def packed(before, middle, after, coef):
        value = coef[3] * middle
        for k in range(7):
            s = k - 3
            if s < 0:
                cell = jnp.where(quarter < -s, left(before, 4 + s), left(middle, s))
            elif s > 0:
                cell = jnp.where(quarter >= 4 - s, left(after, s - 4), left(middle, s))
            else:
                continue
            value += coef[k] * cell
        return value

    change_w = packed(halo_w, own_w, own_w2, betas(c_w, c_w_next))
    change_e = packed(own_e2, own_e, halo_e, betas(c_e, c_e_next))

    for f in range(F):
        value = base[f] - jnp.where(lane < 4, left(change_w, 4 * f), 0.0)
        base[f] = value - jnp.where(lane >= 124, left(change_e, 4 * f + 4), 0.0)

    halo[4].wait()

    @pl.when(z == nz - 1)
    def _():
        clat[:, 8:9, :] = jnp.zeros((L, 1, C), F32)

    for l in range(L):
        for k, coef in enumerate(betas(clat[l, 0:8, :], clat[l, 1:9, :])):
            latw[l, k] = coef

    for copy in halo[2:4]:
        copy.wait()

    @pl.when(z == 0)
    def _():
        field[:, 5:8, :] = jnp.zeros((F, 3, C), F32)

    @pl.when(z == nz - 1)
    def _():
        field[:, 16:19, :] = jnp.zeros((F, 3, C), F32)

    keep = filled[...] < 0.5
    mass_new = [jnp.zeros((R, C), F32) for _ in range(T)]
    for l in range(L):
        coef = [latw[l, k] for k in range(7)]
        kept = jnp.where(keep, mass[l * R : (l + 1) * R, :], 0.0)
        for t in range(T):
            f = t * L + l
            value = base[f]
            for k in range(7):
                value -= coef[k] * field[f, 5 + k : 13 + k, :]
            adv[f * R : (f + 1) * R, :] = value
            mass_new[t] += kept * value

    for r in range(R):
        high, low_part = halves(adv[pl.ds(r, F, stride=R), :])
        at = pl.ds(r * F, F)
        lhs[at, 0:C] = high
        lhs[at, C : 2 * C] = low_part
        lhs[at, 2 * C : 3 * C] = high
    mixed[...] = jnp.dot(lhs[...], colw[...], preferred_element_type=F32)
    for v in range(6):
        total = jnp.zeros((F, C), F32)
        for r in range(R):
            total += roww[r, v : v + 1, :] * mixed[r * F : (r + 1) * F, v * C : (v + 1) * C]
        first, second = total[0 : F // 2, :], total[F // 2 : F, :]
        packet[v] = jnp.where(low16, first, left(second, K))
        packet[v + 6] = jnp.where(low16, left(first, K), second)
    for i in far_first:
        peer = at_z(i)
        remote(packet.at[peer], arrived.at[z], MARGIN, (other, peer, b)).start()

    wait_all(cm_recv, recv_sem.at[MASSES])
    parts = [jnp.zeros((R, C), F32) for _ in range(2)]
    for d in range(12):
        four = cm_recv[d]
        eight = jnp.concatenate([four, left(four, K)], axis=0)
        eight = jnp.where(low, eight, left(eight, K))
        for half in range(2):
            parts[half] += eight * packet[d, half * R : (half + 1) * R, :]
    for half in range(2):
        mass_new[half] += jnp.where(low, parts[half], 0.0)
        mass_new[half + 2] += jnp.where(low, 0.0, parts[half])
    stacked = jnp.concatenate(
        [jnp.sum(m, axis=0, keepdims=True) for m in [mass_old[t] for t in range(T)] + mass_new], axis=0
    )
    sums = jnp.sum(stacked, axis=1, keepdims=True)
    row = jnp.sum(jnp.where(lane == sub[0:R, :], sums, 0.0), axis=0, keepdims=True)

    rows[0:1, :] = row
    rows[3:4, :] = jnp.zeros((1, C), F32)
    for n, (i, j) in enumerate(plane):
        device = (p, z, at_plane(i, j))
        if n < FAR:
            remote(rows.at[pl.ds(0, 1), :], sum_far.at[pl.ds(n, 1), :], SUM_FAR, device).start()

            @pl.when(sends_direct[n])
            def _():
                slot = (z - middle[0]) * 2 + p
                remote(rows.at[pl.ds(0, 1), :], direct.at[slot, pl.ds(n, 1), :], DIRECT, (1, 0, 0)).start()

        else:
            remote(rows.at[pl.ds(0, 1), :], sum_near.at[pl.ds(n - FAR, 1), :], SUM_NEAR, device).start()
    line = [(core, i) for i in far_first if i > 0 for core in (p, other)] + [(other, 0)]
    to_first = [(core == 1) & (b == 0) & (z == nz - i) if i in middle else None for core, i in line]
    wait_all(sum_near, recv_sem.at[SUM_NEAR])
    row = row + jnp.sum(sum_near[...], axis=0, keepdims=True)
    rows[2:3, :] = row

    def along_z(n, source):
        core, i = line[n]
        remote(rows.at[pl.ds(source, 1), :], sum_z.at[pl.ds(n, 1), :], SUM_Z, (core, at_z(i), b)).start()

    @pl.when((b == 0) & in_middle)
    def _():
        for n, special in enumerate(to_first):
            if special is not None:
                pl.when(special)(lambda n=n: along_z(n, 2))

    wait_all(sum_far, recv_sem.at[SUM_FAR])
    row = row + jnp.sum(sum_far[...], axis=0, keepdims=True)
    rows[1:2, :] = row
    for n, special in enumerate(to_first):
        if special is None:
            along_z(n, 1)
        else:
            pl.when(jnp.logical_not(special))(lambda n=n: along_z(n, 1))

    wait_all(arrived, recv_sem.at[MARGIN])
    for v in range(6):
        cols = pl.ds(v * C, C)
        one, two = arrived[v], arrived[v + 6]
        first = jnp.where(low16, one, left(two, K))
        second = jnp.where(low16, left(one, K), two)
        values = jnp.concatenate([first, second], axis=0)
        high = values.astype(BF16).astype(F32)
        low_part = values - high
        for r in range(R):
            at = pl.ds(r * F, F)
            here = live_rows[v] == r
            scat_hi[at, cols] = jnp.where(here, high, 0.0).astype(BF16)
            scat_lo[at, cols] = jnp.where(here, low_part, 0.0).astype(BF16)
    nt = (((1,), (1,)), ((), ()))
    scattered[...] = lax.dot_general(
        scat_hi[...], onehot[...], nt, preferred_element_type=F32
    ) + lax.dot_general(scat_lo[...], onehot[...], nt, preferred_element_type=F32)
    for f in range(F):
        at = pl.ds(f * R, R)
        adv[at, :] = jnp.where(keep, adv[at, :], scattered[pl.ds(f, R, stride=F), :])

    @pl.when(is_first)
    def _():
        wait_all(direct, recv_sem.at[DIRECT])
        rows[3:4, :] = jnp.sum(jnp.sum(direct[...], axis=0), axis=0, keepdims=True)

    wait_all(sum_z, recv_sem.at[SUM_Z])
    row = row + (jnp.sum(sum_z[...], axis=0, keepdims=True) + rows[3:4, :])
    ratio = row / left(row, 4)
    for t in range(T):
        scale = jnp.broadcast_to(ratio[:, t : t + 1], (R, C))
        for l in range(L):
            f = t * L + l
            out[f] = adv[f * R : (f + 1) * R, :] * scale

    wait_all(cm_send, send_sem.at[MASSES])
    wait_all(packet, send_sem.at[MARGIN])
    wait_all(sum_far, send_sem.at[SUM_FAR])
    wait_all(sum_near, send_sem.at[SUM_NEAR])

    @pl.when(direct_any)
    def _():
        wait_all(rows.at[pl.ds(0, 1), :], send_sem.at[DIRECT])

    wait_all(sum_z, send_sem.at[SUM_Z])


def solution(mesh):
    nz, nlon = mesh.shape["lat"], mesh.shape["lon"]
    ny = nlon // NX

    def body(tracers, courant_lon, courant_lat, cell_mass, donor_cell, donor_frac, target_cell, live_count):
        slots = nz * K
        hbm_spec = pl.BlockSpec(memory_space=pltpu.HBM)
        vmem_spec = pl.BlockSpec(memory_space=pltpu.VMEM)

        def run(*refs):
            kernel(nz, nlon, *refs)

        result = pl.pallas_call(
            run,
            out_shape=pltpu.VMEM((F, R, C), F32),
            in_specs=[hbm_spec] * 8,
            out_specs=vmem_spec,
            scratch_shapes=[
                pltpu.VMEM((F, 3 * R, C), F32),
                pltpu.VMEM((L, R, C), F32),
                pltpu.VMEM((L, 2 * R, C), F32),
                pltpu.VMEM((L * R, C), F32),
                pltpu.VMEM((nz, 1, K), jnp.int32),
                pltpu.VMEM((2, nz, 1, K), F32),
                pltpu.VMEM((nz, 1, K), jnp.int32),
                pltpu.SMEM((nz,), jnp.int32),
                pltpu.VMEM((2, R, C), F32),
                pltpu.VMEM((1, R, C), F32),
                pltpu.VMEM((1, R, C), F32),
                pltpu.VMEM((2, R, C), F32),
                pltpu.VMEM((nz, 4, C), F32),
                pltpu.VMEM((nz, 4, C), F32),
                pltpu.VMEM((nz, 2 * R, C), F32),
                pltpu.VMEM((nz, 2 * R, C), F32),
                pltpu.VMEM((4, C), F32),
                pltpu.VMEM((FAR, C), F32),
                pltpu.VMEM((nlon - 1 - FAR, C), F32),
                pltpu.VMEM((2 * (nz - 5), FAR, C), F32),
                pltpu.VMEM((2 * nz - 1, C), F32),
                pltpu.VMEM((8, R, C), F32),
                pltpu.VMEM((R, C), F32),
                pltpu.VMEM((T, R, C), F32),
                pltpu.VMEM((F, R, C), F32),
                pltpu.VMEM((L, 7, R, C), F32),
                pltpu.VMEM((F * R, C), F32),
                pltpu.VMEM((C, slots), BF16),
                pltpu.VMEM((3 * C, slots), BF16),
                pltpu.VMEM((R, R, C), F32),
                pltpu.VMEM((F * R, 3 * C), BF16),
                pltpu.VMEM((F * R, slots), F32),
                pltpu.VMEM((F * R, slots), BF16),
                pltpu.VMEM((F * R, slots), BF16),
                pltpu.VMEM((2 * R, slots), BF16),
                pltpu.VMEM((F * R, C), F32),
                pltpu.SemaphoreType.DMA((8,)),
                pltpu.SemaphoreType.DMA((11,)),
                pltpu.SemaphoreType.DMA((11,)),
            ],
            compiler_params=pltpu.CompilerParams(collective_id=0, has_side_effects=True),
        )(
            tracers.reshape(F, R, C),
            courant_lon.reshape(L, R, C),
            courant_lat.reshape(L, R, C),
            cell_mass.reshape(L * R, C),
            donor_cell.reshape(nz, 1, K),
            donor_frac.reshape(2, nz, 1, K),
            target_cell.reshape(nz, 1, K),
            live_count.reshape(nz),
        )
        return result.reshape(1, T, L, R, C)

    lon = "lon"
    placed = (
        P("panel", None, None, "lat", lon),
        P("panel", None, "lat", lon),
        P("panel", None, "lat", lon),
        P("panel", None, "lat", lon),
        P("panel", "lat", lon, None, None),
        P(None, "panel", "lat", lon, None, None),
        P("panel", "lat", lon, None, None),
        P("panel", "lat", lon, None),
    )
    return jax.shard_map(
        body,
        mesh=mesh,
        in_specs=placed,
        out_specs=P("panel", None, None, "lat", lon),
        check_vma=False,
    )
```

```python
import jax
import jax.numpy as jnp
from jax import lax
from jax.experimental import pallas as pl
from jax.experimental.pallas import tpu as pltpu
from jax.sharding import PartitionSpec as P

F32 = jnp.float32
BF16 = jnp.bfloat16
MESH = pl.DeviceIdType.MESH

T = 4
L = 8
F = T * L
R = 8
C = 128
K = 64
FAR = 12
NX = 4
WEST, EAST, SOUTH, NORTH, NORTH_C, MASSES, MARGIN, SUM_FAR, SUM_NEAR, SUM_Z, DIRECT = range(11)


def left(x, by):
    by = by % C
    return x if by == 0 else pltpu.roll(x, (C - by) % C, x.ndim - 1)


def alphas(c):
    s = jnp.abs(c)
    m = 0.5 * s
    n = m - m * s * (2.0 / 3.0)
    n3 = 3.0 * n
    k1 = c * (1.0 - m - n3)
    k0 = c * (m - n3)
    ka = 2.0 * n3 * c
    u = k0 * (1.0 / 12.0)
    w = k1 * (1.0 / 12.0)
    pos = c > 0.0
    zero = jnp.zeros_like(c)
    near = 7.0 * (u + w) + ka
    far = 7.0 * u - w
    mid = 7.0 * w - u
    return (
        jnp.where(pos, -u, zero),
        jnp.where(pos, far, -w),
        jnp.where(pos, near, mid),
        jnp.where(pos, mid, near),
        jnp.where(pos, -w, far),
        jnp.where(pos, zero, -u),
    )


def betas(c, c_next):
    here, after = alphas(c), alphas(c_next)
    return [-here[0]] + [after[k - 1] - here[k] for k in range(1, 6)] + [after[5]]


def cubic(t):
    a, b, d = t + 1.0, t - 1.0, t - 2.0
    return (
        -t * b * d * (1.0 / 6.0),
        a * b * d * 0.5,
        -a * t * d * 0.5,
        a * t * b * (1.0 / 6.0),
    )


def pick(delta, weights):
    value = jnp.where(delta == 0, weights[0], 0.0)
    for i in range(1, 4):
        value = jnp.where(delta == i, weights[i], value)
    return value


def halves(x):
    high = x.astype(BF16)
    return high, (x - high.astype(F32)).astype(BF16)


def wait_all(ref, sem):
    pltpu.make_async_copy(ref, ref, sem).wait()


def kernel(nz, nlon, q_hbm, clon_hbm, clat_hbm, mass_hbm, donor_hbm, frac_hbm, target_hbm, live_hbm,
           out, field, clon, clat, mass, donor, frac, target, live, send_w, send_e, recv_w, recv_e,
           cm_send, cm_recv, packet, arrived, rows, sum_far, sum_near, direct, sum_z, ends, filled, mass_old, base, latw, adv, onehot, colw,
           roww, lhs, mixed, scat_hi, scat_lo, rowmask, scattered, local_sem, send_sem, recv_sem):
    p = lax.axis_index("panel")
    z = lax.axis_index("lat")
    b = lax.axis_index("lon")
    x, y = lax.rem(b, NX), lax.div(b, NX)
    ny = nlon // NX
    other = 1 - p

    def at_z(step):
        return lax.rem(z + step, nz)

    west, east = lax.rem(b + nlon - 1, nlon), lax.rem(b + 1, nlon)
    south, north = at_z(nz - 1), at_z(1)

    loads = [
        pltpu.make_async_copy(q_hbm, field.at[:, pl.ds(R, R), :], local_sem.at[0]),
        pltpu.make_async_copy(clon_hbm, clon, local_sem.at[1]),
        pltpu.make_async_copy(clat_hbm, clat.at[:, pl.ds(0, R), :], local_sem.at[2]),
        pltpu.make_async_copy(mass_hbm, mass, local_sem.at[3]),
        pltpu.make_async_copy(donor_hbm, donor, local_sem.at[4]),
        pltpu.make_async_copy(frac_hbm, frac, local_sem.at[5]),
        pltpu.make_async_copy(target_hbm, target, local_sem.at[6]),
        pltpu.make_async_copy(live_hbm, live, local_sem.at[7]),
    ]
    barrier = pltpu.get_barrier_semaphore()
    far_first = sorted(range(nz), key=lambda i: -min(i, nz - i))
    partners = [(core, at_z(i), b) for i in far_first[:-1] for core in (other, p)] + [(other, z, b)]
    plane = [(i, j) for i in range(ny) for j in range(NX) if i + j > 0]
    plane.sort(key=lambda ij: -min(ij[0], ny - ij[0]) - min(ij[1], NX - ij[1]))

    def at_plane(i, j):
        return lax.rem(y + i, ny) * NX + lax.rem(x + j, NX)

    partners += [(p, z, at_plane(i, j)) for i, j in plane]
    for load in (loads[6], loads[7], loads[3], *loads[:3], *loads[4:6]):
        load.start()
    middle = range(3, nz - 2)
    is_first = (p == 1) & (z == 0) & (b == 0)
    in_middle = (z >= middle[0]) & (z <= middle[-1])
    sends_direct = [(at_plane(i, j) == 0) & in_middle for i, j in plane[:FAR]]
    direct_any = sends_direct[0]
    for one in sends_direct[1:]:
        direct_any = direct_any | one

    for partner in partners:
        pl.semaphore_signal(barrier, inc=1, device_id=partner, device_id_type=MESH)

    @pl.when(is_first)
    def _():
        for i, j in plane[:FAR]:
            place = (ny - i) % ny * NX + (NX - j) % NX

            @pl.loop(middle[0], middle[-1] + 1)
            def _(level):
                for core in range(2):
                    pl.semaphore_signal(barrier, inc=1, device_id=(core, level, place), device_id_type=MESH)

    lane = lax.broadcasted_iota(jnp.int32, (R, C), 1)
    lane16 = lax.broadcasted_iota(jnp.int32, (2 * R, C), 1)
    lane_row = lax.broadcasted_iota(jnp.int32, (1, C), 1)
    sub = lax.broadcasted_iota(jnp.int32, (2 * R, C), 0)
    column = lax.broadcasted_iota(jnp.int32, (C, C), 0)
    low, low16 = lane < K, lane16 < K

    loads[6].wait()
    loads[7].wait()

    def slots(read):
        return jnp.concatenate(
            [jnp.concatenate([read(v), read(v + 6)], axis=1) for v in range(6)], axis=0
        )

    spots = slots(lambda d: target[d])
    spot_col = spots & (C - 1)
    spot_row = spots >> 7
    live_rows = []
    for v in range(6):
        count = jnp.where(lane_row < K, live[v], live[v + 6])
        live_rows.append(jnp.where((lane_row & (K - 1)) < count, spot_row[v : v + 1, :], R))
    for v in range(6):
        cols = pl.ds(v * C, C)
        onehot[:, cols] = jnp.where(column == spot_col[v : v + 1, :], 1.0, 0.0).astype(BF16)

    loads[3].wait()
    by_row = jnp.concatenate([mass[pl.ds(r, L, stride=R), :] for r in range(R)], axis=0)
    mass_hi, mass_lo = halves(by_row)
    mass_at = jnp.dot(mass_hi, onehot[...], preferred_element_type=F32) + jnp.dot(
        mass_lo, onehot[...], preferred_element_type=F32
    )
    for v in range(6):
        total = jnp.zeros((L, C), F32)
        for r in range(R):
            total += jnp.where(
                live_rows[v] == r, mass_at[r * L : (r + 1) * L, v * C : (v + 1) * C], 0.0
            )
        turned = left(total, K)
        cm_send[v] = jnp.where(low, total, pltpu.roll(turned, 4, 0))[0:4, :]
        cm_send[v + 6] = jnp.where(low, turned, pltpu.roll(total, 4, 0))[0:4, :]

    loads[0].wait()
    loads[1].wait()
    loads[2].wait()

    def pack_ends():
        own = [jnp.zeros((R, C), F32) for _ in range(4)]
        firsts = (0, 4, 124, 120)
        for f in range(F):
            tile = field[f, R : 2 * R, :]
            band = (lane >= 4 * f) & (lane < 4 * f + 4)
            own = [jnp.where(band, left(tile, first - 4 * f), o) for first, o in zip(firsts, own)]
        edge = [jnp.zeros((R, C), F32) for _ in range(4)]
        firsts = (0, 1, 124, 125)
        for l in range(L):
            tile = clon[l]
            band = (lane >= 4 * l) & (lane < 4 * l + 4)
            edge = [jnp.where(band, left(tile, first - 4 * l), o) for first, o in zip(firsts, edge)]
        edge = [o + pltpu.roll(o, 32, 1) for o in edge]
        edge = [o + pltpu.roll(o, 64, 1) for o in edge]
        for n, tile in enumerate(own + edge):
            ends[n] = tile
        send_w[0] = own[0]
        send_w[1] = edge[0]
        send_e[0] = own[2]

    def prepare():
        loads[4].wait()
        loads[5].wait()
        cells = slots(lambda d: donor[d])
        start_col = cells & (C - 1)
        start_row = cells >> 7
        row_weights = cubic(slots(lambda d: frac[0, d]))
        col_weights = cubic(slots(lambda d: frac[1, d]))
        for r in range(R):
            roww[r, 0:6, :] = pick(r - start_row, row_weights)
        for v in range(6):
            cols = pl.ds(v * C, C)
            weights = pick(
                column - start_col[v : v + 1, :], [w[v : v + 1, :] for w in col_weights]
            )
            high, low_part = halves(weights)
            colw[0:C, cols] = high
            colw[C : 2 * C, cols] = high
            colw[2 * C : 3 * C, cols] = low_part

        for v in range(6):
            rowmask[:, pl.ds(v * C, C)] = jnp.where(sub == live_rows[v], 1.0, 0.0).astype(BF16)
        filled[...] = lax.dot_general(
            rowmask[...], onehot[...], (((1,), (1,)), ((), ())), preferred_element_type=F32
        )[0:R, :]

        inside = (lane >= 4) & (lane < 124)
        old = [jnp.zeros((R, C), F32) for _ in range(T)]
        for l in range(L):
            coef = [
                jnp.where(inside, o, 0.0) for o in betas(clon[l], left(clon[l], 1))
            ]
            for t in range(T):
                tile = field[t * L + l, R : 2 * R, :]
                old[t] += mass[l * R : (l + 1) * R, :] * tile
                value = tile
                for k in range(7):
                    value -= coef[k] * left(tile, k - 3)
                base[t * L + l] = value
        for t in range(T):
            mass_old[t] = old[t]

    pack_ends()

    late = (z >= nz - 2) & (y >= ny // 2) & (y < ny - 1)
    pl.when(jnp.logical_not(late))(prepare)
    pl.semaphore_wait(barrier, len(partners) + jnp.where(direct_any, 1, 0))

    def remote(src, dst, which, device):
        return pltpu.make_async_remote_copy(
            src_ref=src,
            dst_ref=dst,
            send_sem=send_sem.at[which],
            recv_sem=recv_sem.at[which],
            device_id=device,
            device_id_type=MESH,
        )

    far_first = sorted(range(nz), key=lambda i: -min(i, nz - i))
    halo = [
        remote(send_w, recv_e, EAST, (p, z, west)),
        remote(send_e, recv_w, WEST, (p, z, east)),
        remote(field.at[:, pl.ds(13, 3), :], field.at[:, pl.ds(5, 3), :], SOUTH, (p, north, b)),
        remote(field.at[:, pl.ds(8, 3), :], field.at[:, pl.ds(16, 3), :], NORTH, (p, south, b)),
        remote(clat.at[:, pl.ds(0, 1), :], clat.at[:, pl.ds(R, 1), :], NORTH_C, (p, south, b)),
    ]
    def send_masses(steps):
        for i in steps:
            peer = at_z(i)
            remote(cm_send.at[peer], cm_recv.at[z], MASSES, (other, peer, b)).start()

    def start(copies):
        for copy in copies:
            copy.start()

    start(halo[:2])
    send_masses(far_first[:5])
    start(halo[2:])
    send_masses(far_first[5:])
    pl.when(late)(prepare)

    for copy in halo[:2]:
        copy.wait()
    own_w, own_w2, own_e, own_e2, c_w, c_w_next, c_e, c_e_next = (ends[n] for n in range(8))
    quarter = lane & 3
    halo_w = jnp.where(b == 0, 0.0, recv_w[0])
    halo_e = jnp.where(b == nlon - 1, 0.0, recv_e[0])
    halo_c = jnp.where(b == nlon - 1, 0.0, recv_e[1])
    c_e_next = jnp.where(quarter == 3, left(halo_c, -3), c_e_next)

    def packed(before, middle, after, coef):
        value = coef[3] * middle
        for k in range(7):
            s = k - 3
            if s < 0:
                cell = jnp.where(quarter < -s, left(before, 4 + s), left(middle, s))
            elif s > 0:
                cell = jnp.where(quarter >= 4 - s, left(after, s - 4), left(middle, s))
            else:
                continue
            value += coef[k] * cell
        return value

    change_w = packed(halo_w, own_w, own_w2, betas(c_w, c_w_next))
    change_e = packed(own_e2, own_e, halo_e, betas(c_e, c_e_next))

    for f in range(F):
        value = base[f] - jnp.where(lane < 4, left(change_w, 4 * f), 0.0)
        base[f] = value - jnp.where(lane >= 124, left(change_e, 4 * f + 4), 0.0)

    halo[4].wait()

    @pl.when(z == nz - 1)
    def _():
        clat[:, 8:9, :] = jnp.zeros((L, 1, C), F32)

    for l in range(L):
        for k, coef in enumerate(betas(clat[l, 0:8, :], clat[l, 1:9, :])):
            latw[l, k] = coef

    for copy in halo[2:4]:
        copy.wait()

    @pl.when(z == 0)
    def _():
        field[:, 5:8, :] = jnp.zeros((F, 3, C), F32)

    @pl.when(z == nz - 1)
    def _():
        field[:, 16:19, :] = jnp.zeros((F, 3, C), F32)

    keep = filled[...] < 0.5
    mass_new = [jnp.zeros((R, C), F32) for _ in range(T)]
    for l in range(L):
        coef = [latw[l, k] for k in range(7)]
        kept = jnp.where(keep, mass[l * R : (l + 1) * R, :], 0.0)
        for t in range(T):
            f = t * L + l
            value = base[f]
            for k in range(7):
                value -= coef[k] * field[f, 5 + k : 13 + k, :]
            adv[f * R : (f + 1) * R, :] = value
            mass_new[t] += kept * value

    for r in range(R):
        high, low_part = halves(adv[pl.ds(r, F, stride=R), :])
        at = pl.ds(r * F, F)
        lhs[at, 0:C] = high
        lhs[at, C : 2 * C] = low_part
        lhs[at, 2 * C : 3 * C] = high
    mixed[...] = jnp.dot(lhs[...], colw[...], preferred_element_type=F32)
    for v in range(6):
        total = jnp.zeros((F, C), F32)
        for r in range(R):
            total += roww[r, v : v + 1, :] * mixed[r * F : (r + 1) * F, v * C : (v + 1) * C]
        first, second = total[0 : F // 2, :], total[F // 2 : F, :]
        packet[v] = jnp.where(low16, first, left(second, K))
        packet[v + 6] = jnp.where(low16, left(first, K), second)
    for i in far_first:
        peer = at_z(i)
        remote(packet.at[peer], arrived.at[z], MARGIN, (other, peer, b)).start()

    def spread(stacked, first):
        sums = jnp.sum(stacked, axis=1, keepdims=True)
        count = stacked.shape[0]
        return jnp.sum(
            jnp.where(lane[0:count, :] == sub[0:count, :] + first, sums, 0.0), axis=0, keepdims=True
        )

    masses = [mass_old[t] for t in range(T)] + mass_new
    rows[2:3, :] = spread(
        jnp.concatenate([jnp.sum(m, axis=0, keepdims=True) for m in masses], axis=0), 0
    )

    wait_all(cm_recv, recv_sem.at[MASSES])
    parts = [jnp.zeros((R, C), F32) for _ in range(2)]
    for d in range(12):
        four = cm_recv[d]
        eight = jnp.concatenate([four, left(four, K)], axis=0)
        eight = jnp.where(low, eight, left(eight, K))
        for half in range(2):
            parts[half] += eight * packet[d, half * R : (half + 1) * R, :]
    parts = [jnp.sum(part, axis=0, keepdims=True) for part in parts]
    halved = [jnp.where(lane_row < K, part, 0.0) for part in parts]
    halved += [jnp.where(lane_row < K, 0.0, part) for part in parts]
    row = rows[2:3, :] + spread(jnp.concatenate(halved, axis=0), T)

    rows[0:1, :] = row
    rows[3:4, :] = jnp.zeros((1, C), F32)
    for n, (i, j) in enumerate(plane):
        device = (p, z, at_plane(i, j))
        if n < FAR:
            remote(rows.at[pl.ds(0, 1), :], sum_far.at[pl.ds(n, 1), :], SUM_FAR, device).start()

            @pl.when(sends_direct[n])
            def _():
                slot = (z - middle[0]) * 2 + p
                remote(rows.at[pl.ds(0, 1), :], direct.at[slot, pl.ds(n, 1), :], DIRECT, (1, 0, 0)).start()

        else:
            remote(rows.at[pl.ds(0, 1), :], sum_near.at[pl.ds(n - FAR, 1), :], SUM_NEAR, device).start()
    line = [(core, i) for i in far_first if i > 0 for core in (p, other)] + [(other, 0)]
    to_first = [(core == 1) & (b == 0) & (z == nz - i) if i in middle else None for core, i in line]
    wait_all(sum_near, recv_sem.at[SUM_NEAR])
    row = row + jnp.sum(sum_near[...], axis=0, keepdims=True)
    rows[2:3, :] = row

    def along_z(n, source):
        core, i = line[n]
        remote(rows.at[pl.ds(source, 1), :], sum_z.at[pl.ds(n, 1), :], SUM_Z, (core, at_z(i), b)).start()

    @pl.when((b == 0) & in_middle)
    def _():
        for n, special in enumerate(to_first):
            if special is not None:
                pl.when(special)(lambda n=n: along_z(n, 2))

    wait_all(sum_far, recv_sem.at[SUM_FAR])
    row = row + jnp.sum(sum_far[...], axis=0, keepdims=True)
    rows[1:2, :] = row
    for n, special in enumerate(to_first):
        if special is None:
            along_z(n, 1)
        else:
            pl.when(jnp.logical_not(special))(lambda n=n: along_z(n, 1))

    wait_all(arrived, recv_sem.at[MARGIN])
    for v in range(6):
        cols = pl.ds(v * C, C)
        one, two = arrived[v], arrived[v + 6]
        first = jnp.where(low16, one, left(two, K))
        second = jnp.where(low16, left(one, K), two)
        values = jnp.concatenate([first, second], axis=0)
        high = values.astype(BF16).astype(F32)
        low_part = values - high
        for r in range(R):
            at = pl.ds(r * F, F)
            here = live_rows[v] == r
            scat_hi[at, cols] = jnp.where(here, high, 0.0).astype(BF16)
            scat_lo[at, cols] = jnp.where(here, low_part, 0.0).astype(BF16)
    nt = (((1,), (1,)), ((), ()))
    scattered[...] = lax.dot_general(
        scat_hi[...], onehot[...], nt, preferred_element_type=F32
    ) + lax.dot_general(scat_lo[...], onehot[...], nt, preferred_element_type=F32)
    for f in range(F):
        at = pl.ds(f * R, R)
        adv[at, :] = jnp.where(keep, adv[at, :], scattered[pl.ds(f, R, stride=F), :])

    @pl.when(is_first)
    def _():
        wait_all(direct, recv_sem.at[DIRECT])
        rows[3:4, :] = jnp.sum(jnp.sum(direct[...], axis=0), axis=0, keepdims=True)

    wait_all(sum_z, recv_sem.at[SUM_Z])
    row = row + (jnp.sum(sum_z[...], axis=0, keepdims=True) + rows[3:4, :])
    ratio = row / left(row, 4)
    for t in range(T):
        scale = jnp.broadcast_to(ratio[:, t : t + 1], (R, C))
        for l in range(L):
            f = t * L + l
            out[f] = adv[f * R : (f + 1) * R, :] * scale

    wait_all(cm_send, send_sem.at[MASSES])
    wait_all(packet, send_sem.at[MARGIN])
    wait_all(sum_far, send_sem.at[SUM_FAR])
    wait_all(sum_near, send_sem.at[SUM_NEAR])

    @pl.when(direct_any)
    def _():
        wait_all(rows.at[pl.ds(0, 1), :], send_sem.at[DIRECT])

    wait_all(sum_z, send_sem.at[SUM_Z])


def solution(mesh):
    nz, nlon = mesh.shape["lat"], mesh.shape["lon"]
    ny = nlon // NX

    def body(tracers, courant_lon, courant_lat, cell_mass, donor_cell, donor_frac, target_cell, live_count):
        slots = nz * K
        hbm_spec = pl.BlockSpec(memory_space=pltpu.HBM)
        vmem_spec = pl.BlockSpec(memory_space=pltpu.VMEM)

        def run(*refs):
            kernel(nz, nlon, *refs)

        result = pl.pallas_call(
            run,
            out_shape=pltpu.VMEM((F, R, C), F32),
            in_specs=[hbm_spec] * 8,
            out_specs=vmem_spec,
            scratch_shapes=[
                pltpu.VMEM((F, 3 * R, C), F32),
                pltpu.VMEM((L, R, C), F32),
                pltpu.VMEM((L, 2 * R, C), F32),
                pltpu.VMEM((L * R, C), F32),
                pltpu.VMEM((nz, 1, K), jnp.int32),
                pltpu.VMEM((2, nz, 1, K), F32),
                pltpu.VMEM((nz, 1, K), jnp.int32),
                pltpu.SMEM((nz,), jnp.int32),
                pltpu.VMEM((2, R, C), F32),
                pltpu.VMEM((1, R, C), F32),
                pltpu.VMEM((1, R, C), F32),
                pltpu.VMEM((2, R, C), F32),
                pltpu.VMEM((nz, 4, C), F32),
                pltpu.VMEM((nz, 4, C), F32),
                pltpu.VMEM((nz, 2 * R, C), F32),
                pltpu.VMEM((nz, 2 * R, C), F32),
                pltpu.VMEM((4, C), F32),
                pltpu.VMEM((FAR, C), F32),
                pltpu.VMEM((nlon - 1 - FAR, C), F32),
                pltpu.VMEM((2 * (nz - 5), FAR, C), F32),
                pltpu.VMEM((2 * nz - 1, C), F32),
                pltpu.VMEM((8, R, C), F32),
                pltpu.VMEM((R, C), F32),
                pltpu.VMEM((T, R, C), F32),
                pltpu.VMEM((F, R, C), F32),
                pltpu.VMEM((L, 7, R, C), F32),
                pltpu.VMEM((F * R, C), F32),
                pltpu.VMEM((C, slots), BF16),
                pltpu.VMEM((3 * C, slots), BF16),
                pltpu.VMEM((R, R, C), F32),
                pltpu.VMEM((F * R, 3 * C), BF16),
                pltpu.VMEM((F * R, slots), F32),
                pltpu.VMEM((F * R, slots), BF16),
                pltpu.VMEM((F * R, slots), BF16),
                pltpu.VMEM((2 * R, slots), BF16),
                pltpu.VMEM((F * R, C), F32),
                pltpu.SemaphoreType.DMA((8,)),
                pltpu.SemaphoreType.DMA((11,)),
                pltpu.SemaphoreType.DMA((11,)),
            ],
            compiler_params=pltpu.CompilerParams(collective_id=0, has_side_effects=True),
        )(
            tracers.reshape(F, R, C),
            courant_lon.reshape(L, R, C),
            courant_lat.reshape(L, R, C),
            cell_mass.reshape(L * R, C),
            donor_cell.reshape(nz, 1, K),
            donor_frac.reshape(2, nz, 1, K),
            target_cell.reshape(nz, 1, K),
            live_count.reshape(nz),
        )
        return result.reshape(1, T, L, R, C)

    lon = "lon"
    placed = (
        P("panel", None, None, "lat", lon),
        P("panel", None, "lat", lon),
        P("panel", None, "lat", lon),
        P("panel", None, "lat", lon),
        P("panel", "lat", lon, None, None),
        P(None, "panel", "lat", lon, None, None),
        P("panel", "lat", lon, None, None),
        P("panel", "lat", lon, None),
    )
    return jax.shard_map(
        body,
        mesh=mesh,
        in_specs=placed,
        out_specs=P("panel", None, None, "lat", lon),
        check_vma=False,
    )
```
